512 devices in a mesh: blk: 128 (over z, y, core), dir: 4 (over x).
Axes of the slice: x: 4, y: 8, z: 8, core: 2. Of those that a mesh axis runs over, the one named last changes fastest.
Arguments:
- spectrum: float32 [36, 36, 2048, 128], P('dir', None, 'blk'), may hold values from 0 to 4.5, as said below
- group_speed: float32 [36, 2048, 128], P(None, 'blk'), may hold values from 0.3 to 1
- ocean_current: float32 [2, 128, 2048], P(None, 'blk'), may hold values from -0.5 to 0.5
- route_slot: int32 [2048, 128], P('blk'), may hold values from -1 to 2047, as said below
- wind_vector: float32 [128, 2, 2048], P('blk'), may hold values from -4 to 4
- ice_cover: float32 [128, 2048], P('blk'), may hold values from 0 to 0.9
Outputs:
- spectrum_out: float32 [36, 36, 2048, 128], P('dir', None, 'blk')
- ocean_forcing: float32 [4, 128, 2048], P('dir', 'blk')
The draws below stay inside these ranges and needn't reach their ends.
Inputs may be any that keep to these rules, and one draw needn't show every extreme that they name: `route_slot`: on one geographic block the sea cells routed to one owner use slots 0 to their count - 1, at most 16 of them; some owner receives 16 cells from every block. Land cells hold -1. `spectrum`: positive everywhere.
All inputs are finite; a program needn't handle non-finite values.
Results may differ from the reference program's by a relative error of at most 0.00002.
Values sent between devices are 32-bit elements; how exact they have to be, the bound alone decides.
No kernel may reach another device: no remote copies, remote signals or barrier semaphores. Data moves between devices by JAX's collectives and lax.ppermute only.
A program may use at most 64 MiB of HBM per device.

```python
import math
import jax
import jax.numpy as jnp
from jax import lax

DIRS = 36
FREQS = 36
GY = 128
CX = 16
BLOCKS = 128
NX = 2048
CAP = 16
SLOTS = 2048


def draw_spectrum(key, part):
    cell_key, element_key = jax.random.split(jax.random.fold_in(key, 23))
    ramp = jnp.arange(DIRS, dtype=jnp.float32) / (DIRS - 1)
    cell_scale = jnp.exp(jax.random.uniform(cell_key, (NX, GY), jnp.float32, 0.0, math.log(10.0))) / 10.0
    element = jnp.exp(jax.random.uniform(element_key, (DIRS, FREQS, NX, GY), jnp.float32, math.log(0.1), 0.0))
    band = (1.0 + 2.0 * ramp)[:, None] * jnp.ones((FREQS,), jnp.float32)[None, :]
    return (band[:, :, None, None] * cell_scale[None, None] * element).astype(jnp.float32)


def draw_route_slot(key, part):
    target_key, block_keys = jax.random.split(jax.random.fold_in(key, 11))
    target = jax.random.randint(target_key, (), 0, BLOCKS)
    cell_count = CX * GY
    owners = jnp.arange(BLOCKS, dtype=jnp.int32)

    def one_block(block_index):
        block_key = jax.random.fold_in(block_keys, block_index)
        count_key, order_key = jax.random.split(block_key)
        counts = jax.random.randint(count_key, (BLOCKS,), 1, CAP + 1)
        counts = jnp.where(owners == target, CAP, counts).astype(jnp.int32)
        upper = jnp.cumsum(counts).astype(jnp.int32)
        lower = upper - counts
        ranks = jax.random.permutation(order_key, cell_count).astype(jnp.int32)
        owner = jnp.sum((ranks[:, None] >= upper[None, :]).astype(jnp.int32), axis=1)
        start = jnp.sum(jnp.where(owners[None, :] == owner[:, None], lower[None, :], 0), axis=1)
        routed = jnp.where(ranks < upper[BLOCKS - 1], owner * CAP + ranks - start, -1)
        return routed.reshape(CX, GY).astype(jnp.int32)
    return lax.map(one_block, owners).reshape(BLOCKS * CX, GY).astype(jnp.int32)


def shard_levels(key, shape, pieces, low, top_value):
    def one(dim, shards_of):
        steps = jax.random.uniform(jax.random.fold_in(jax.random.fold_in(key, 6), dim), (shards_of,), jnp.float32, low / len(pieces), top_value / len(pieces))
        return jnp.repeat(jnp.exp(steps), shape[dim] // shards_of).reshape((-1,) + (1,) * (len(shape) - dim - 1))

    factor_of = one(*pieces[0])
    for cut in pieces[1:]:
        factor_of = factor_of * one(*cut)
    return factor_of


def centred(stream_key, extent, spread, bound, pieces=(), kind=jnp.bfloat16):
    entries = jax.random.normal(stream_key, extent, jnp.float32) * spread
    if len(pieces) > 0:
        entries = shard_levels(stream_key, extent, pieces, -0.22, 0.18) * entries
    return jnp.clip(entries, min=-bound, max=bound).astype(kind)


def setup_inputs(seed: int = 0) -> dict:
    seeds = jax.random.split(jax.random.key(seed), 7)
    spectrum = draw_spectrum(jax.random.fold_in(seeds[6], 71), 0)
    group_speed = jnp.clip(0.3 + 0.7 * jax.random.uniform(seeds[1], (FREQS, NX, GY), jnp.float32) ** shard_levels(seeds[1], (FREQS, NX, GY), ((1, 128),), -0.2, 0.2), 0.3, 1.0)
    ocean_current = jnp.clip(jax.random.uniform(seeds[2], (2, GY, NX), jnp.float32, -0.5, 0.5) * shard_levels(seeds[2], (2, GY, NX), ((1, 128),), -0.4, 0.0), -0.5, 0.5)
    route_slot = draw_route_slot(jax.random.fold_in(seeds[6], 71), 0)
    wind_vector = centred(seeds[4], (BLOCKS, 2, SLOTS), 1.0, 4.0, ((0, 128),), jnp.float32)
    ice_cover = jnp.clip(0.9 * jax.random.uniform(seeds[5], (BLOCKS, SLOTS), jnp.float32) ** shard_levels(seeds[5], (BLOCKS, SLOTS), ((0, 128),), -0.2, 0.2), 0.0, 0.9)
    return {"spectrum": spectrum, "group_speed": group_speed, "ocean_current": ocean_current, "route_slot": route_slot, "wind_vector": wind_vector, "ice_cover": ice_cover}


COURANT = 0.15
WIND_GROWTH = 0.15
DAMP_RATE = 0.5
STEEP_COEF = 0.01
STRESS_SCALE = 1.0
STOKES_SCALE = 0.15
RATIO_STEP = 1.1


def flux_difference(energy, velocity, open_mask, along):
    count = energy.shape[along] - 1
    low_energy = lax.slice_in_dim(energy, 0, count, axis=along)
    high_energy = lax.slice_in_dim(energy, 1, count + 1, axis=along)
    face_speed = 0.5 * (lax.slice_in_dim(velocity, 0, count, axis=along) + lax.slice_in_dim(velocity, 1, count + 1, axis=along))
    face_open = lax.slice_in_dim(open_mask, 0, count, axis=along) * lax.slice_in_dim(open_mask, 1, count + 1, axis=along)
    flux = face_open * (jnp.maximum(face_speed, 0.0) * low_energy + jnp.minimum(face_speed, 0.0) * high_energy)
    return lax.slice_in_dim(flux, 1, count, axis=along) - lax.slice_in_dim(flux, 0, count - 1, axis=along)


def pad_edges(array, along):
    widths = [(0, 0)] * array.ndim
    widths[along] = (1, 1)
    return jnp.pad(array, widths)


def reference(spectrum, group_speed, ocean_current, route_slot, wind_vector, ice_cover):
    currents = jnp.transpose(ocean_current, (0, 2, 1))
    sea_mask = (route_slot >= 0).astype(jnp.float32)
    safe_slot = jnp.where(route_slot >= 0, route_slot, 0).astype(jnp.int32)
    owner = (safe_slot // CAP).astype(jnp.int32)
    column = ((jnp.arange(NX, dtype=jnp.int32) // CX)[:, None] * CAP + safe_slot % CAP).astype(jnp.int32)
    wind_cell = jnp.moveaxis(wind_vector[owner, :, column], -1, 0)
    ice_cell = ice_cover[owner, column]
    ratios = jnp.power(jnp.float32(RATIO_STEP), jnp.arange(FREQS, dtype=jnp.float32) - (FREQS - 1))
    ratio_square = ratios * ratios
    ratio_cube = ratio_square * ratios
    angles = 2.0 * jnp.pi * jnp.arange(DIRS, dtype=jnp.float32) / DIRS
    cosine_dir = jnp.cos(angles)
    sine_dir = jnp.sin(angles)

    def advect(inputs):
        energy, cosine, sine = inputs
        velocity_x = group_speed * cosine + currents[0]
        velocity_y = group_speed * sine + currents[1]
        mask_full = jnp.broadcast_to(sea_mask, energy.shape)
        div_x = flux_difference(pad_edges(energy, 1), pad_edges(velocity_x, 1), pad_edges(mask_full, 1), 1)
        div_y = flux_difference(pad_edges(energy, 2), pad_edges(velocity_y, 2), pad_edges(mask_full, 2), 2)
        return sea_mask * (energy - COURANT * (div_x + div_y))

    moved = lax.map(advect, (spectrum, cosine_dir, sine_dir))
    moment = jnp.sum(moved * ratio_square[None, :, None, None], axis=(0, 1))
    steepness = STEEP_COEF * moment
    damping = DAMP_RATE * steepness / (1.0 + steepness)

    def source(inputs):
        energy, cosine, sine = inputs
        wind_gain = WIND_GROWTH * (1.0 - ice_cell) * jnp.maximum(wind_cell[0] * cosine + wind_cell[1] * sine, 0.0)
        growth = ratios[:, None, None] * (wind_gain - damping)[None]
        updated = energy * (1.0 + growth)
        stress = jnp.sum(ratio_square[:, None, None] * wind_gain[None] * energy, axis=0)
        stokes = jnp.sum(ratio_cube[:, None, None] * updated, axis=0)
        return updated, stress, stokes

    updated, stress, stokes = lax.map(source, (moved, cosine_dir, sine_dir))
    cosine_full = cosine_dir[:, None, None]
    sine_full = sine_dir[:, None, None]
    forcing = jnp.stack([
        STRESS_SCALE * jnp.sum(cosine_full * stress, axis=0),
        STRESS_SCALE * jnp.sum(sine_full * stress, axis=0),
        STOKES_SCALE * jnp.sum(cosine_full * stokes, axis=0),
        STOKES_SCALE * jnp.sum(sine_full * stokes, axis=0)])
    return updated, jnp.transpose(forcing, (0, 2, 1))
```

```python
import jax
import jax.numpy as jnp
import numpy as np
from jax import lax
from jax.experimental import pallas as pl
from jax.experimental.pallas import tpu as pltpu
from jax.sharding import PartitionSpec as P

BLK = "blk"
DIR = "dir"
VMEM = pltpu.VMEM
SMEM = pltpu.SMEM

COURANT = 0.15
WIND_GROWTH = 0.15
DAMP_RATE = 0.5
STEEP_COEF = 0.01
STOKES_SCALE = 0.15
RATIO_STEP = 1.1

LANES = 128
ROWS = 16
CUR_X, CUR_Y, WIND_X, WIND_Y, ICE = 0, 24, 48, 64, 80


def vmem_specs(count):
    return [pl.BlockSpec(memory_space=VMEM)] * count


def lane_of(shape):
    return lax.broadcasted_iota(jnp.int32, shape, len(shape) - 1)


def message_kernel(cur_ref, wind_ref, ice_ref, out_ref, x_ref):
    for c in range(2):
        for r in range(ROWS):
            x_ref[c, r : r + 1, :] = wind_ref[c : c + 1, LANES * r : LANES * (r + 1)]
    lane = lane_of((ROWS, LANES))

    def put(s, values, start):
        return pltpu.roll(values, (start - ROWS * s) % LANES, 1)

    for s in range(8):
        row = jnp.where(lane < CUR_Y, put(s, cur_ref[0], CUR_X + 1), put(s, cur_ref[1], CUR_Y))
        row = jnp.where(lane < WIND_X, row, put(s, x_ref[0], WIND_X))
        row = jnp.where(lane < WIND_Y, row, put(s, x_ref[1], WIND_Y))
        row = jnp.where(lane < ICE, row, put(s, ice_ref[...], ICE))
        out_ref[pl.ds(s, ROWS, stride=8), :] = row
    whole = out_ref[...]
    wide = lane_of((LANES, LANES))
    before = pltpu.roll(pltpu.roll(whole, 1, 0), LANES - ROWS, 1)
    after = pltpu.roll(pltpu.roll(whole, LANES - 1, 0), ROWS, 1)
    whole = jnp.where(wide == CUR_X, before, whole)
    out_ref[...] = jnp.where(wide == CUR_X + ROWS + 1, after, whole)


def edge_kernel(bins, freqs, spec_ref, speed_ref, slot_ref, last_ref, first_ref):
    for out_ref, row in ((last_ref, ROWS - 1), (first_ref, 0)):
        out_ref[0:bins, :] = spec_ref[pl.ds(row, bins, stride=ROWS), :]
        out_ref[bins : bins + freqs, :] = speed_ref[pl.ds(row, freqs, stride=ROWS), :]
        sea = jnp.where(slot_ref[row : row + 1, :] >= 0, 1.0, 0.0)
        out_ref[bins + freqs :, :] = jnp.broadcast_to(sea, (8, LANES))


def move_kernel(
    dirs,
    freqs,
    at_ref,
    trig_ref,
    got_ref,
    spec_ref,
    speed_ref,
    low_ref,
    high_ref,
    slot_ref,
    moved_ref,
    parts_ref,
    cell_ref,
    turned_ref,
    sx_ref,
    sy_ref,
    s16_ref,
    f16_ref,
):
    shape = (ROWS, LANES)
    row, lane = lax.broadcasted_iota(jnp.int32, shape, 0), lane_of(shape)
    bins = dirs * freqs
    turned_ref[...] = got_ref[...].T

    def shifted_down(values, first):
        return jnp.where(row == 0, jnp.broadcast_to(first, shape), pltpu.roll(values, 1, 0))

    def next_y(values):
        return pltpu.roll(values, LANES - 1, 1)

    slots = slot_ref[...]
    sea = jnp.where(slots >= 0, 1.0, 0.0)
    sea_low, sea_high = low_ref[bins + freqs : bins + freqs + 1, :], high_ref[bins + freqs : bins + freqs + 1, :]
    half = 0.5 * COURANT
    open_x = half * sea * shifted_down(sea, sea_low)
    open_y = jnp.where(lane < LANES - 1, half * sea * next_y(sea), 0.0)
    open_16 = half * sea[ROWS - 1 : ROWS, :] * sea_high
    flow_x = open_x * (turned_ref[CUR_X : CUR_X + ROWS, :] + turned_ref[CUR_X + 1 : CUR_X + ROWS + 1, :])
    flow_16 = open_16 * (turned_ref[CUR_X + ROWS : CUR_X + ROWS + 1, :] + turned_ref[CUR_X + ROWS + 1 : CUR_X + ROWS + 2, :])
    cur_y = turned_ref[CUR_Y : CUR_Y + ROWS, :]
    flow_y = open_y * (cur_y + next_y(cur_y))

    owner, place = jnp.maximum(slots, 0) // 16, jnp.where(slots >= 0, slots % 16, -1)
    wind_x, wind_y, ice = (jnp.zeros(shape, jnp.float32) for _ in range(3))
    for s in range(16):
        here = place == s

        def picked(start, old):
            table = jnp.broadcast_to(turned_ref[start + s : start + s + 1, :], shape)
            return jnp.where(here, jnp.take_along_axis(table, owner, axis=1), old)

        wind_x, wind_y, ice = picked(WIND_X, wind_x), picked(WIND_Y, wind_y), picked(ICE, ice)
    gain = WIND_GROWTH * (1.0 - ice)
    cell_ref[0:16, :] = wind_x
    cell_ref[16:32, :] = wind_y
    cell_ref[32:48, :] = gain

    def faces(k, _):
        base = pl.multiple_of(k * ROWS, ROWS)
        speed = speed_ref[pl.ds(base, ROWS), :]
        sx_ref[pl.ds(base, ROWS), :] = open_x * (speed + shifted_down(speed, low_ref[pl.ds(bins + k, 1), :]))
        sy_ref[pl.ds(base, ROWS), :] = open_y * (speed + next_y(speed))
        return 0

    lax.fori_loop(0, freqs, faces, 0, unroll=4)
    s16_ref[...] = open_16 * (speed_ref[pl.ds(ROWS - 1, freqs, stride=ROWS), :] + high_ref[bins : bins + freqs, :])

    zero = jnp.zeros(shape, jnp.float32)
    moment, stress_x, stress_y, drift_x, drift_y, damp_x, damp_y = (zero,) * 7
    at = at_ref[0]
    for j in range(dirs):
        cosine, sine = trig_ref[at, j], trig_ref[at, dirs + j]
        face = s16_ref[...] * cosine + flow_16
        f16_ref[...] = face * jnp.where(
            face > 0.0,
            spec_ref[pl.ds(j * freqs * ROWS + ROWS - 1, freqs, stride=ROWS), :],
            high_ref[j * freqs : (j + 1) * freqs, :],
        )

        def step(k, sums):
            second, third, fourth = sums
            base = pl.multiple_of(k * ROWS, ROWS)
            here = pl.multiple_of(j * freqs * ROWS + k * ROWS, ROWS)
            energy = spec_ref[pl.ds(here, ROWS), :]
            u = sx_ref[pl.ds(base, ROWS), :] * cosine + flow_x
            below = u * jnp.where(u > 0.0, shifted_down(energy, low_ref[pl.ds(j * freqs + k, 1), :]), energy)
            above = jnp.where(
                row == ROWS - 1, jnp.broadcast_to(f16_ref[pl.ds(k, 1), :], shape), pltpu.roll(below, ROWS - 1, 0)
            )
            v = sy_ref[pl.ds(base, ROWS), :] * sine + flow_y
            right = v * jnp.where(v > 0.0, energy, next_y(energy))
            left = pltpu.roll(right, 1, 1)
            moved = sea * (energy - ((above - below) + (right - left)))
            moved_ref[pl.ds(here, ROWS), :] = moved
            return (
                second * (RATIO_STEP**-2) + moved,
                third * (RATIO_STEP**-3) + moved,
                fourth * (RATIO_STEP**-4) + moved,
            )

        second, third, fourth = lax.fori_loop(0, freqs, step, (zero, zero, zero), unroll=4)
        wind_gain = gain * jnp.maximum(wind_x * cosine + wind_y * sine, 0.0)
        push = wind_gain * second
        drift = third + wind_gain * fourth
        moment += second
        stress_x += cosine * push
        stress_y += sine * push
        drift_x += cosine * drift
        drift_y += sine * drift
        damp_x += cosine * fourth
        damp_y += sine * fourth
    for c, (main, damped) in enumerate(((stress_x, zero), (stress_y, zero), (drift_x, damp_x), (drift_y, damp_y))):
        parts_ref[c, 0:16, :] = moment
        parts_ref[c, 16:32, :] = main
        parts_ref[c, 32:48, :] = damped


def forcing_kernel(at_ref, parts_ref, damping_ref, out_ref):
    parts = (parts_ref[0] + parts_ref[1]) + (parts_ref[2] + parts_ref[3])
    steepness = STEEP_COEF * parts[0:16]
    damping = DAMP_RATE * steepness / (1.0 + steepness)
    damping_ref[...] = damping
    own = parts[16:32] - damping * parts[32:48]
    own = jnp.where(at_ref[0] < 2, 1.0, STOKES_SCALE) * own
    out_ref[...] = jnp.concatenate([own, jnp.zeros((LANES - ROWS, LANES), jnp.float32)], axis=0).T


def update_kernel(dirs, freqs, at_ref, trig_ref, moved_ref, cell_ref, damping_ref, out_ref):
    j, at = pl.program_id(0), at_ref[0]
    cosine, sine = trig_ref[at, j], trig_ref[at, dirs + j]
    wind = jnp.maximum(cell_ref[0:16, :] * cosine + cell_ref[16:32, :] * sine, 0.0)
    growth = cell_ref[32:48, :] * wind - damping_ref[...]
    start = pl.multiple_of(j * freqs * ROWS, ROWS)
    for k in range(freqs):
        ratio = RATIO_STEP ** (k - freqs + 1)
        out_ref[k * ROWS : (k + 1) * ROWS, :] = moved_ref[pl.ds(start + k * ROWS, ROWS), :] * (1.0 + ratio * growth)


def row_kernel(got_ref, out_ref):
    lane = lane_of((ROWS, LANES))
    row = got_ref[pl.ds(0, ROWS, stride=8), :]
    for s in range(1, 8):
        row = jnp.where(lane < ROWS * s, row, pltpu.roll(got_ref[pl.ds(s, ROWS, stride=8), :], ROWS * s, 1))
    out_ref[...] = row


def f32(*shape):
    return jax.ShapeDtypeStruct(shape, jnp.float32)


def on_device(spectrum, group_speed, ocean_current, route_slot, wind_vector, ice_cover):
    dirs, freqs, _, _ = spectrum.shape
    bands, blocks = lax.axis_size(DIR), lax.axis_size(BLK)
    bins = dirs * freqs
    at = lax.axis_index(DIR).astype(jnp.int32).reshape(1)
    angles = (2.0 * np.pi * np.arange(bands * dirs, dtype=np.float32) / np.float32(bands * dirs)).astype(np.float32)
    angles = angles.astype(np.float64).reshape(bands, dirs)
    trig = jnp.asarray(np.concatenate([np.cos(angles), np.sin(angles)], axis=1).astype(np.float32))
    smem = pl.BlockSpec(memory_space=SMEM)

    messages = pl.pallas_call(
        message_kernel,
        out_shape=f32(LANES, LANES),
        in_specs=vmem_specs(3),
        out_specs=vmem_specs(1)[0],
        scratch_shapes=[VMEM((2, ROWS, LANES), jnp.float32)],
        name="messages",
    )(
        ocean_current.reshape(2, ROWS, LANES),
        wind_vector.reshape(2, ROWS * LANES),
        ice_cover.reshape(ROWS, LANES),
    )
    got = lax.all_to_all(messages, BLK, 0, 0, tiled=True)

    flat = spectrum.reshape(bins * ROWS, LANES)
    speed = group_speed.reshape(freqs * ROWS, LANES)
    edge = f32(bins + freqs + 8, LANES)
    last, first = pl.pallas_call(
        lambda *refs: edge_kernel(bins, freqs, *refs),
        out_shape=(edge, edge),
        in_specs=vmem_specs(3),
        out_specs=tuple(vmem_specs(2)),
        name="edges",
    )(flat, speed, route_slot)
    up = [(i, i + 1) for i in range(blocks - 1)]
    low = lax.ppermute(last, BLK, up)
    high = lax.ppermute(first, BLK, [(j, i) for i, j in up])

    moved, parts, cell = pl.pallas_call(
        lambda *refs: move_kernel(dirs, freqs, *refs),
        out_shape=(f32(bins * ROWS, LANES), f32(bands, 48, LANES), f32(48, LANES)),
        in_specs=[smem, smem] + vmem_specs(6),
        out_specs=tuple(vmem_specs(3)),
        scratch_shapes=[
            VMEM((LANES, LANES), jnp.float32),
            VMEM((freqs * ROWS, LANES), jnp.float32),
            VMEM((freqs * ROWS, LANES), jnp.float32),
            VMEM((freqs, LANES), jnp.float32),
            VMEM((freqs, LANES), jnp.float32),
        ],
        name="move",
    )(at, trig, got, flat, speed, low, high, route_slot)

    parts = lax.all_to_all(parts, DIR, 0, 0, tiled=True)
    damping, own = pl.pallas_call(
        forcing_kernel,
        out_shape=(f32(ROWS, LANES), f32(LANES, LANES)),
        in_specs=[smem] + vmem_specs(1),
        out_specs=tuple(vmem_specs(2)),
        name="forcing",
    )(at, parts)
    ocean = lax.all_to_all(own, BLK, 0, 0, tiled=True)
    result = pl.pallas_call(
        lambda *refs: update_kernel(dirs, freqs, *refs),
        out_shape=f32(bins * ROWS, LANES),
        grid=(dirs,),
        in_specs=[smem, smem] + vmem_specs(3),
        out_specs=pl.BlockSpec((freqs * ROWS, LANES), lambda j: (j, 0)),
        name="update",
        cost_estimate=pl.CostEstimate(flops=3 * bins * ROWS * LANES, bytes_accessed=8 * bins * ROWS * LANES, transcendentals=0),
    )(at, trig, moved, cell, damping)
    ocean = pl.pallas_call(
        row_kernel,
        out_shape=f32(ROWS, LANES),
        in_specs=vmem_specs(1),
        out_specs=vmem_specs(1)[0],
        name="rows",
    )(ocean)
    return (result.reshape(spectrum.shape), ocean.reshape(1, 1, ROWS * LANES))


def solution(mesh):
    return jax.shard_map(
        on_device,
        mesh=mesh,
        in_specs=(
            P(DIR, None, BLK, None),
            P(None, BLK, None),
            P(None, BLK, None),
            P(BLK, None),
            P(BLK, None, None),
            P(BLK, None),
        ),
        out_specs=(P(DIR, None, BLK, None), P(DIR, BLK, None)),
        check_vma=False,
    )
```

```python
import jax
import jax.numpy as jnp
import numpy as np
from jax import lax
from jax.experimental import pallas as pl
from jax.experimental.pallas import tpu as pltpu
from jax.sharding import PartitionSpec as P


BLK = "blk"
DIR = "dir"
VMEM = pltpu.VMEM
SMEM = pltpu.SMEM

COURANT = 0.15
WIND_GROWTH = 0.15
DAMP_RATE = 0.5
STEEP_COEF = 0.01
STOKES_SCALE = 0.15
RATIO_STEP = 1.1

LANES = 128
MIB = 1 << 20
UNROLL = 18
ROWS = 16
CUR_X, CUR_Y, WIND_X, WIND_Y, ICE = 0, 24, 48, 64, 80


def vmem_specs(count):
    return [pl.BlockSpec(memory_space=VMEM)] * count


def lane_of(shape):
    return lax.broadcasted_iota(jnp.int32, shape, len(shape) - 1)


def message_kernel(cur_ref, wind_ref, ice_ref, out_ref, x_ref):
    for c in range(2):
        for r in range(ROWS):
            x_ref[c, r : r + 1, :] = wind_ref[c : c + 1, LANES * r : LANES * (r + 1)]
    lane = lane_of((ROWS, LANES))

    def put(s, values, start):
        return pltpu.roll(values, (start - ROWS * s) % LANES, 1)

    for s in range(8):
        row = jnp.where(lane < CUR_Y, put(s, cur_ref[0], CUR_X + 1), put(s, cur_ref[1], CUR_Y))
        row = jnp.where(lane < WIND_X, row, put(s, x_ref[0], WIND_X))
        row = jnp.where(lane < WIND_Y, row, put(s, x_ref[1], WIND_Y))
        row = jnp.where(lane < ICE, row, put(s, ice_ref[...], ICE))
        out_ref[pl.ds(s, ROWS, stride=8), :] = row
    whole = out_ref[...]
    wide = lane_of((LANES, LANES))
    before = pltpu.roll(pltpu.roll(whole, 1, 0), LANES - ROWS, 1)
    after = pltpu.roll(pltpu.roll(whole, LANES - 1, 0), ROWS, 1)
    whole = jnp.where(wide == CUR_X, before, whole)
    out_ref[...] = jnp.where(wide == CUR_X + ROWS + 1, after, whole)


def edge_kernel(bins, freqs, spec_ref, speed_ref, slot_ref, last_ref, first_ref):
    for out_ref, row in ((last_ref, ROWS - 1), (first_ref, 0)):
        out_ref[0:bins, :] = spec_ref[pl.ds(row, bins, stride=ROWS), :]
        out_ref[bins : bins + freqs, :] = speed_ref[pl.ds(row, freqs, stride=ROWS), :]
        sea = jnp.where(slot_ref[row : row + 1, :] >= 0, 1.0, 0.0)
        out_ref[bins + freqs :, :] = jnp.broadcast_to(sea, (8, LANES))


def move_kernel(
    dirs,
    freqs,
    at_ref,
    trig_ref,
    got_ref,
    spec_ref,
    speed_ref,
    low_ref,
    high_ref,
    slot_ref,
    stored_ref,
    parts_ref,
    cell_ref,
    turned_ref,
    sx_ref,
    sy_ref,
    sw_ref,
    s16_ref,
    f16_ref,
    moved_ref,
    sems,
):
    shape = (ROWS, LANES)
    row, lane = lax.broadcasted_iota(jnp.int32, shape, 0), lane_of(shape)
    bins = dirs * freqs
    turned_ref[...] = got_ref[...].T

    def shifted_down(values, first):
        return jnp.where(row == 0, jnp.broadcast_to(first, shape), pltpu.roll(values, 1, 0))

    def next_y(values):
        return pltpu.roll(values, LANES - 1, 1)

    slots = slot_ref[...]
    sea = jnp.where(slots >= 0, 1.0, 0.0)
    sea_low, sea_high = low_ref[bins + freqs : bins + freqs + 1, :], high_ref[bins + freqs : bins + freqs + 1, :]
    half = 0.5 * COURANT
    open_x = half * sea * shifted_down(sea, sea_low)
    open_y = jnp.where(lane < LANES - 1, half * sea * next_y(sea), 0.0)
    open_16 = half * sea[ROWS - 1 : ROWS, :] * sea_high
    flow_x = open_x * (turned_ref[CUR_X : CUR_X + ROWS, :] + turned_ref[CUR_X + 1 : CUR_X + ROWS + 1, :])
    flow_16 = open_16 * (turned_ref[CUR_X + ROWS : CUR_X + ROWS + 1, :] + turned_ref[CUR_X + ROWS + 1 : CUR_X + ROWS + 2, :])
    cur_y = turned_ref[CUR_Y : CUR_Y + ROWS, :]
    flow_y = open_y * (cur_y + next_y(cur_y))
    flow_w = pltpu.roll(flow_y, 1, 1)

    owner, place = jnp.maximum(slots, 0) // 16, jnp.where(slots >= 0, slots % 16, -1)
    wind_x, wind_y, ice = (jnp.zeros(shape, jnp.float32) for _ in range(3))
    for s in range(16):
        here = place == s

        def picked(start, old):
            table = jnp.broadcast_to(turned_ref[start + s : start + s + 1, :], shape)
            return jnp.where(here, jnp.take_along_axis(table, owner, axis=1), old)

        wind_x, wind_y, ice = picked(WIND_X, wind_x), picked(WIND_Y, wind_y), picked(ICE, ice)
    gain = WIND_GROWTH * (1.0 - ice)
    cell_ref[0:16, :] = wind_x
    cell_ref[16:32, :] = wind_y
    cell_ref[32:48, :] = gain

    def faces(k, _):
        base = pl.multiple_of(k * ROWS, ROWS)
        speed = speed_ref[pl.ds(base, ROWS), :]
        sx_ref[pl.ds(base, ROWS), :] = open_x * (speed + shifted_down(speed, low_ref[pl.ds(bins + k, 1), :]))
        side = open_y * (speed + next_y(speed))
        sy_ref[pl.ds(base, ROWS), :] = side
        sw_ref[pl.ds(base, ROWS), :] = pltpu.roll(side, 1, 1)
        return 0

    lax.fori_loop(0, freqs, faces, 0, unroll=12)
    s16_ref[...] = open_16 * (speed_ref[pl.ds(ROWS - 1, freqs, stride=ROWS), :] + high_ref[bins : bins + freqs, :])

    zero = jnp.zeros(shape, jnp.float32)
    moment, stress_x, stress_y, drift_x, drift_y, damp_x, damp_y = (zero,) * 7
    at = at_ref[0]
    copies = []
    for j in range(dirs):
        cosine, sine = trig_ref[at, j], trig_ref[at, dirs + j]
        face = s16_ref[...] * cosine + flow_16
        f16_ref[...] = face * jnp.where(
            face > 0.0,
            spec_ref[pl.ds(j * freqs * ROWS + ROWS - 1, freqs, stride=ROWS), :],
            high_ref[j * freqs : (j + 1) * freqs, :],
        )

        def step(k, sums):
            second, third, fourth = sums
            base = pl.multiple_of(k * ROWS, ROWS)
            here = pl.multiple_of(j * freqs * ROWS + k * ROWS, ROWS)
            energy = spec_ref[pl.ds(here, ROWS), :]
            u = sx_ref[pl.ds(base, ROWS), :] * cosine + flow_x
            below = u * jnp.where(u > 0.0, shifted_down(energy, low_ref[pl.ds(j * freqs + k, 1), :]), energy)
            above = jnp.where(
                row == ROWS - 1, jnp.broadcast_to(f16_ref[pl.ds(k, 1), :], shape), pltpu.roll(below, ROWS - 1, 0)
            )
            v = sy_ref[pl.ds(base, ROWS), :] * sine + flow_y
            right = v * jnp.where(v > 0.0, energy, next_y(energy))
            w = sw_ref[pl.ds(base, ROWS), :] * sine + flow_w
            left = w * jnp.where(w > 0.0, pltpu.roll(energy, 1, 1), energy)
            moved = sea * (energy - ((above - below) + (right - left)))
            moved_ref[pl.ds(here, ROWS), :] = moved
            return (
                second * (RATIO_STEP**-2) + moved,
                third * (RATIO_STEP**-3) + moved,
                fourth * (RATIO_STEP**-4) + moved,
            )

        def out_copy():
            part = pl.ds(j * freqs * ROWS, freqs * ROWS)
            return pltpu.make_async_copy(moved_ref.at[part, :], stored_ref.at[part, :], sems.at[j])

        second, third, fourth = lax.fori_loop(0, freqs, step, (zero, zero, zero), unroll=UNROLL)
        copies.append(out_copy())
        copies[-1].start()
        wind_gain = gain * jnp.maximum(wind_x * cosine + wind_y * sine, 0.0)
        push = wind_gain * second
        drift = third + wind_gain * fourth
        moment += second
        stress_x += cosine * push
        stress_y += sine * push
        drift_x += cosine * drift
        drift_y += sine * drift
        damp_x += cosine * fourth
        damp_y += sine * fourth
    for c, (main, damped) in enumerate(((stress_x, zero), (stress_y, zero), (drift_x, damp_x), (drift_y, damp_y))):
        parts_ref[c, 0:16, :] = moment
        parts_ref[c, 16:32, :] = main
        parts_ref[c, 32:48, :] = damped
    for copy in copies:
        copy.wait()


def forcing_kernel(at_ref, parts_ref, damping_ref, out_ref):
    parts = (parts_ref[0] + parts_ref[1]) + (parts_ref[2] + parts_ref[3])
    steepness = STEEP_COEF * parts[0:16]
    damping = DAMP_RATE * steepness / (1.0 + steepness)
    damping_ref[...] = damping
    own = parts[16:32] - damping * parts[32:48]
    own = jnp.where(at_ref[0] < 2, 1.0, STOKES_SCALE) * own
    out_ref[...] = jnp.concatenate([own, jnp.zeros((LANES - ROWS, LANES), jnp.float32)], axis=0).T


def update_kernel(dirs, freqs, at_ref, trig_ref, moved_ref, cell_ref, damping_ref, out_ref):
    j, at = pl.program_id(0), at_ref[0]
    cosine, sine = trig_ref[at, j], trig_ref[at, dirs + j]
    wind = jnp.maximum(cell_ref[0:16, :] * cosine + cell_ref[16:32, :] * sine, 0.0)
    growth = cell_ref[32:48, :] * wind - damping_ref[...]
    for k in range(freqs):
        ratio = RATIO_STEP ** (k - freqs + 1)
        out_ref[k * ROWS : (k + 1) * ROWS, :] = moved_ref[k * ROWS : (k + 1) * ROWS, :] * (1.0 + ratio * growth)


def row_kernel(got_ref, out_ref):
    lane = lane_of((ROWS, LANES))
    row = got_ref[pl.ds(0, ROWS, stride=8), :]
    for s in range(1, 8):
        row = jnp.where(lane < ROWS * s, row, pltpu.roll(got_ref[pl.ds(s, ROWS, stride=8), :], ROWS * s, 1))
    out_ref[...] = row


def f32(*shape):
    return jax.ShapeDtypeStruct(shape, jnp.float32)


def near(*shape):
    return VMEM(shape, jnp.float32)


def held(value):
    return pltpu.with_memory_space_constraint(value, VMEM)


def one_step(spectrum, group_speed, ocean_current, route_slot, wind_vector, ice_cover):
    dirs, freqs, _, _ = spectrum.shape
    bands, blocks = lax.axis_size(DIR), lax.axis_size(BLK)
    bins = dirs * freqs
    at = lax.axis_index(DIR).astype(jnp.int32).reshape(1)
    angles = (2.0 * np.pi * np.arange(bands * dirs, dtype=np.float32) / np.float32(bands * dirs)).astype(np.float32)
    angles = angles.astype(np.float64).reshape(bands, dirs)
    trig = jnp.asarray(np.concatenate([np.cos(angles), np.sin(angles)], axis=1).astype(np.float32))
    smem = pl.BlockSpec(memory_space=SMEM)

    messages = pl.pallas_call(
        message_kernel,
        out_shape=near(LANES, LANES),
        in_specs=vmem_specs(3),
        out_specs=vmem_specs(1)[0],
        scratch_shapes=[VMEM((2, ROWS, LANES), jnp.float32)],
        name="messages",
        compiler_params=pltpu.CompilerParams(vmem_limit_bytes=4 * MIB),
    )(
        ocean_current.reshape(2, ROWS, LANES),
        wind_vector.reshape(2, ROWS * LANES),
        ice_cover.reshape(ROWS, LANES),
    )
    got = held(lax.all_to_all(messages, BLK, 0, 0, tiled=True))

    flat = held(spectrum.reshape(bins * ROWS, LANES))
    speed = held(group_speed.reshape(freqs * ROWS, LANES))
    edge = near(bins + freqs + 8, LANES)
    edges = pl.pallas_call(
        lambda *refs: edge_kernel(bins, freqs, *refs),
        out_shape=(edge, edge),
        in_specs=vmem_specs(3),
        out_specs=tuple(vmem_specs(2)),
        name="edges",
        compiler_params=pltpu.CompilerParams(vmem_limit_bytes=4 * MIB),
    )
    last, first = edges(flat, speed, route_slot)
    up = [(i, i + 1) for i in range(blocks - 1)]
    low = held(lax.ppermute(last, BLK, up))
    high = held(lax.ppermute(first, BLK, [(j, i) for i, j in up]))

    moved, parts, cell = pl.pallas_call(
        lambda *refs: move_kernel(dirs, freqs, *refs),
        out_shape=(pltpu.HBM((bins * ROWS, LANES), jnp.float32), near(bands, 48, LANES), near(48, LANES)),
        in_specs=[smem, smem] + vmem_specs(6),
        out_specs=(pl.BlockSpec(memory_space=pltpu.HBM), *vmem_specs(2)),
        scratch_shapes=[
            VMEM((LANES, LANES), jnp.float32),
            VMEM((freqs * ROWS, LANES), jnp.float32),
            VMEM((freqs * ROWS, LANES), jnp.float32),
            VMEM((freqs * ROWS, LANES), jnp.float32),
            VMEM((freqs, LANES), jnp.float32),
            VMEM((freqs, LANES), jnp.float32),
            VMEM((bins * ROWS, LANES), jnp.float32),
            pltpu.SemaphoreType.DMA((dirs,)),
        ],
        name="move",
        compiler_params=pltpu.CompilerParams(vmem_limit_bytes=8 * MIB),
    )(at, trig, got, flat, speed, low, high, route_slot)

    parts = held(lax.all_to_all(parts, DIR, 0, 0, tiled=True))
    damping, own = pl.pallas_call(
        forcing_kernel,
        out_shape=(near(ROWS, LANES), near(LANES, LANES)),
        in_specs=[smem] + vmem_specs(1),
        out_specs=tuple(vmem_specs(2)),
        name="forcing",
        compiler_params=pltpu.CompilerParams(vmem_limit_bytes=4 * MIB),
    )(at, parts)
    ocean = held(lax.all_to_all(own, BLK, 0, 0, tiled=True))
    result = pl.pallas_call(
        lambda *refs: update_kernel(dirs, freqs, *refs),
        out_shape=f32(bins * ROWS, LANES),
        grid=(dirs,),
        in_specs=[smem, smem, pl.BlockSpec((freqs * ROWS, LANES), lambda j: (j, 0))] + vmem_specs(2),
        out_specs=pl.BlockSpec((freqs * ROWS, LANES), lambda j: (j, 0)),
        name="update",
        compiler_params=pltpu.CompilerParams(vmem_limit_bytes=4 * MIB),
        cost_estimate=pl.CostEstimate(flops=3 * bins * ROWS * LANES, bytes_accessed=8 * bins * ROWS * LANES, transcendentals=0),
    )(at, trig, pltpu.with_memory_space_constraint(moved, pltpu.HBM), cell, damping)
    ocean = pl.pallas_call(
        row_kernel,
        out_shape=f32(ROWS, LANES),
        in_specs=vmem_specs(1),
        out_specs=vmem_specs(1)[0],
        name="rows",
        compiler_params=pltpu.CompilerParams(vmem_limit_bytes=4 * MIB),
    )(ocean)
    return (result.reshape(spectrum.shape), ocean.reshape(1, 1, ROWS * LANES))


def solution(mesh):
    return jax.shard_map(
        one_step,
        mesh=mesh,
        in_specs=(
            P(DIR, None, BLK, None),
            P(None, BLK, None),
            P(None, BLK, None),
            P(BLK, None),
            P(BLK, None, None),
            P(BLK, None),
        ),
        out_specs=(P(DIR, None, BLK, None), P(DIR, BLK, None)),
        check_vma=False,
    )
```

```python
import jax
import jax.numpy as jnp
import numpy as np
from jax import lax
from jax.experimental import pallas as pl
from jax.experimental.pallas import tpu as pltpu
from jax.sharding import PartitionSpec as P


BLK = "blk"
DIR = "dir"
VMEM = pltpu.VMEM
SMEM = pltpu.SMEM

COURANT = 0.15
WIND_GROWTH = 0.15
DAMP_RATE = 0.5
STEEP_COEF = 0.01
STOKES_SCALE = 0.15
RATIO_STEP = 1.1

LANES = 128
BANDS = 4
MIB = 1 << 20
UNROLL = 18
ROWS = 16
CUR_X, CUR_Y, WIND_X, WIND_Y, ICE = 0, 24, 48, 64, 80


def vmem_specs(count):
    return [pl.BlockSpec(memory_space=VMEM)] * count


def lane_of(shape):
    return lax.broadcasted_iota(jnp.int32, shape, len(shape) - 1)


def outgoing_kernel(
    bins,
    freqs,
    at_ref,
    cur_hbm,
    wind_hbm,
    ice_hbm,
    spec_hbm,
    speed_hbm,
    slot_hbm,
    out_ref,
    pair_ref,
    next_ref,
    cur_ref,
    wind_ref,
    ice_ref,
    spec_ref,
    speed_ref,
    slot_ref,
    x_ref,
    sems,
):
    sources = (cur_hbm, wind_hbm, ice_hbm, slot_hbm, speed_hbm, spec_hbm)
    targets = (cur_ref, wind_ref, ice_ref, slot_ref, speed_ref, spec_ref)
    copies = [pltpu.make_async_copy(a, b, sems.at[i]) for i, (a, b) in enumerate(zip(sources, targets))]
    for copy in copies:
        copy.start()
    for copy in copies[:3]:
        copy.wait()
    for c in range(2):
        for r in range(ROWS):
            x_ref[c, r : r + 1, :] = wind_ref[c : c + 1, LANES * r : LANES * (r + 1)]
    lane = lane_of((ROWS, LANES))

    def put(s, values, start):
        return pltpu.roll(values, (start - ROWS * s) % LANES, 1)

    for s in range(8):
        row = jnp.where(lane < CUR_Y, put(s, cur_ref[0], CUR_X + 1), put(s, cur_ref[1], CUR_Y))
        row = jnp.where(lane < WIND_X, row, put(s, x_ref[0], WIND_X))
        row = jnp.where(lane < WIND_Y, row, put(s, x_ref[1], WIND_Y))
        row = jnp.where(lane < ICE, row, put(s, ice_ref[...], ICE))
        out_ref[pl.ds(s, ROWS, stride=8), :] = row
    whole = out_ref[...]
    wide = lane_of((LANES, LANES))
    before = pltpu.roll(pltpu.roll(whole, 1, 0), LANES - ROWS, 1)
    after = pltpu.roll(pltpu.roll(whole, LANES - 1, 0), ROWS, 1)
    whole = jnp.where(wide == CUR_X, before, whole)
    out_ref[...] = jnp.where(wide == CUR_X + ROWS + 1, after, whole)
    odd = at_ref[0] >= BANDS
    for copy in copies[3:]:
        copy.wait()

    def trade(start, stop, first, last):
        pair_ref[start:stop, :] = jnp.where(odd, first, last)
        next_ref[start:stop, :] = jnp.where(odd, last, first)

    for source, start, count in ((spec_ref, 0, bins), (speed_ref, bins, freqs)):
        trade(start, start + count, source[pl.ds(0, count, stride=ROWS), :], source[pl.ds(ROWS - 1, count, stride=ROWS), :])
    sea = jnp.where(slot_ref[...] >= 0, 1.0, 0.0)
    sea = [jnp.broadcast_to(sea[r : r + 1, :], (8, LANES)) for r in (0, ROWS - 1)]
    trade(bins + freqs, bins + freqs + 8, *sea)


def move_kernel(
    dirs,
    freqs,
    at_ref,
    trig_ref,
    got_ref,
    spec_ref,
    speed_ref,
    pair_ref,
    next_ref,
    slot_ref,
    stored_ref,
    parts_ref,
    cell_ref,
    turned_ref,
    sx_ref,
    sy_ref,
    sw_ref,
    s16_ref,
    f16_ref,
    moved_ref,
    low_ref,
    high_ref,
    sems,
):
    shape = (ROWS, LANES)
    row, lane = lax.broadcasted_iota(jnp.int32, shape, 0), lane_of(shape)
    bins = dirs * freqs
    turned_ref[...] = got_ref[...].T
    odd = at_ref[0] >= BANDS
    low_ref[...] = jnp.where(odd, pair_ref[...], next_ref[...])
    high_ref[...] = jnp.where(odd, next_ref[...], pair_ref[...])

    def shifted_down(values, first):
        return jnp.where(row == 0, jnp.broadcast_to(first, shape), pltpu.roll(values, 1, 0))

    def next_y(values):
        return pltpu.roll(values, LANES - 1, 1)

    slots = slot_ref[...]
    sea = jnp.where(slots >= 0, 1.0, 0.0)
    sea_low, sea_high = low_ref[bins + freqs : bins + freqs + 1, :], high_ref[bins + freqs : bins + freqs + 1, :]
    half = 0.5 * COURANT
    open_x = half * sea * shifted_down(sea, sea_low)
    open_y = jnp.where(lane < LANES - 1, half * sea * next_y(sea), 0.0)
    open_16 = half * sea[ROWS - 1 : ROWS, :] * sea_high
    flow_x = open_x * (turned_ref[CUR_X : CUR_X + ROWS, :] + turned_ref[CUR_X + 1 : CUR_X + ROWS + 1, :])
    flow_16 = open_16 * (turned_ref[CUR_X + ROWS : CUR_X + ROWS + 1, :] + turned_ref[CUR_X + ROWS + 1 : CUR_X + ROWS + 2, :])
    cur_y = turned_ref[CUR_Y : CUR_Y + ROWS, :]
    flow_y = open_y * (cur_y + next_y(cur_y))
    flow_w = pltpu.roll(flow_y, 1, 1)

    owner, place = jnp.maximum(slots, 0) // 16, jnp.where(slots >= 0, slots % 16, -1)
    wind_x, wind_y, ice = (jnp.zeros(shape, jnp.float32) for _ in range(3))
    for s in range(16):
        here = place == s

        def picked(start, old):
            table = jnp.broadcast_to(turned_ref[start + s : start + s + 1, :], shape)
            return jnp.where(here, jnp.take_along_axis(table, owner, axis=1), old)

        wind_x, wind_y, ice = picked(WIND_X, wind_x), picked(WIND_Y, wind_y), picked(ICE, ice)
    gain = WIND_GROWTH * (1.0 - ice)
    cell_ref[0:16, :] = wind_x
    cell_ref[16:32, :] = wind_y
    cell_ref[32:48, :] = gain

    def faces(k, _):
        base = pl.multiple_of(k * ROWS, ROWS)
        speed = speed_ref[pl.ds(base, ROWS), :]
        sx_ref[pl.ds(base, ROWS), :] = open_x * (speed + shifted_down(speed, low_ref[pl.ds(bins + k, 1), :]))
        side = open_y * (speed + next_y(speed))
        sy_ref[pl.ds(base, ROWS), :] = side
        sw_ref[pl.ds(base, ROWS), :] = pltpu.roll(side, 1, 1)
        return 0

    lax.fori_loop(0, freqs, faces, 0, unroll=12)
    s16_ref[...] = open_16 * (speed_ref[pl.ds(ROWS - 1, freqs, stride=ROWS), :] + high_ref[bins : bins + freqs, :])

    zero = jnp.zeros(shape, jnp.float32)
    moment, stress_x, stress_y, drift_x, drift_y, damp_x, damp_y = (zero,) * 7
    at = at_ref[0] % BANDS
    copies = []
    for j in range(dirs):
        cosine, sine = trig_ref[at, j], trig_ref[at, dirs + j]
        face = s16_ref[...] * cosine + flow_16
        f16_ref[...] = face * jnp.where(
            face > 0.0,
            spec_ref[pl.ds(j * freqs * ROWS + ROWS - 1, freqs, stride=ROWS), :],
            high_ref[j * freqs : (j + 1) * freqs, :],
        )

        def step(k, sums):
            second, third, fourth = sums
            base = pl.multiple_of(k * ROWS, ROWS)
            here = pl.multiple_of(j * freqs * ROWS + k * ROWS, ROWS)
            energy = spec_ref[pl.ds(here, ROWS), :]
            u = sx_ref[pl.ds(base, ROWS), :] * cosine + flow_x
            below = u * jnp.where(u > 0.0, shifted_down(energy, low_ref[pl.ds(j * freqs + k, 1), :]), energy)
            above = jnp.where(
                row == ROWS - 1, jnp.broadcast_to(f16_ref[pl.ds(k, 1), :], shape), pltpu.roll(below, ROWS - 1, 0)
            )
            v = sy_ref[pl.ds(base, ROWS), :] * sine + flow_y
            right = v * jnp.where(v > 0.0, energy, next_y(energy))
            w = sw_ref[pl.ds(base, ROWS), :] * sine + flow_w
            left = w * jnp.where(w > 0.0, pltpu.roll(energy, 1, 1), energy)
            moved = sea * (energy - ((above - below) + (right - left)))
            moved_ref[pl.ds(here, ROWS), :] = moved
            return (
                second * (RATIO_STEP**-2) + moved,
                third * (RATIO_STEP**-3) + moved,
                fourth * (RATIO_STEP**-4) + moved,
            )

        def out_copy():
            part = pl.ds(j * freqs * ROWS, freqs * ROWS)
            return pltpu.make_async_copy(moved_ref.at[part, :], stored_ref.at[part, :], sems.at[j])

        second, third, fourth = lax.fori_loop(0, freqs, step, (zero, zero, zero), unroll=UNROLL)
        copies.append(out_copy())
        copies[-1].start()
        wind_gain = gain * jnp.maximum(wind_x * cosine + wind_y * sine, 0.0)
        push = wind_gain * second
        drift = third + wind_gain * fourth
        moment += second
        stress_x += cosine * push
        stress_y += sine * push
        drift_x += cosine * drift
        drift_y += sine * drift
        damp_x += cosine * fourth
        damp_y += sine * fourth
    for c, (main, damped) in enumerate(((stress_x, zero), (stress_y, zero), (drift_x, damp_x), (drift_y, damp_y))):
        parts_ref[c, 0:16, :] = moment
        parts_ref[c, 16:32, :] = main
        parts_ref[c, 32:48, :] = damped
    for copy in copies:
        copy.wait()


def forcing_kernel(at_ref, parts_ref, damping_ref, out_ref):
    parts = (parts_ref[0] + parts_ref[1]) + (parts_ref[2] + parts_ref[3])
    steepness = STEEP_COEF * parts[0:16]
    damping = DAMP_RATE * steepness / (1.0 + steepness)
    damping_ref[...] = damping
    own = parts[16:32] - damping * parts[32:48]
    own = jnp.where(at_ref[0] % BANDS < 2, 1.0, STOKES_SCALE) * own
    out_ref[...] = jnp.concatenate([own, jnp.zeros((LANES - ROWS, LANES), jnp.float32)], axis=0).T


def update_kernel(dirs, freqs, at_ref, trig_ref, moved_ref, cell_ref, damping_ref, out_ref):
    j, at = pl.program_id(0), at_ref[0] % BANDS
    cosine, sine = trig_ref[at, j], trig_ref[at, dirs + j]
    wind = jnp.maximum(cell_ref[0:16, :] * cosine + cell_ref[16:32, :] * sine, 0.0)
    growth = cell_ref[32:48, :] * wind - damping_ref[...]
    for k in range(freqs):
        ratio = RATIO_STEP ** (k - freqs + 1)
        out_ref[k * ROWS : (k + 1) * ROWS, :] = moved_ref[k * ROWS : (k + 1) * ROWS, :] * (1.0 + ratio * growth)


def row_kernel(got_ref, out_ref):
    lane = lane_of((ROWS, LANES))
    row = got_ref[pl.ds(0, ROWS, stride=8), :]
    for s in range(1, 8):
        row = jnp.where(lane < ROWS * s, row, pltpu.roll(got_ref[pl.ds(s, ROWS, stride=8), :], ROWS * s, 1))
    out_ref[...] = row


def f32(*shape):
    return jax.ShapeDtypeStruct(shape, jnp.float32)


def near(*shape):
    return VMEM(shape, jnp.float32)


def held(value):
    return pltpu.with_memory_space_constraint(value, VMEM)


def one_step(spectrum, group_speed, ocean_current, route_slot, wind_vector, ice_cover):
    dirs, freqs, _, _ = spectrum.shape
    bands, blocks = lax.axis_size(DIR), lax.axis_size(BLK)
    bins = dirs * freqs
    at = (lax.axis_index(DIR) + bands * (lax.axis_index(BLK) & 1)).astype(jnp.int32).reshape(1)
    angles = (2.0 * np.pi * np.arange(bands * dirs, dtype=np.float32) / np.float32(bands * dirs)).astype(np.float32)
    angles = angles.astype(np.float64).reshape(bands, dirs)
    trig = jnp.asarray(np.concatenate([np.cos(angles), np.sin(angles)], axis=1).astype(np.float32))
    smem = pl.BlockSpec(memory_space=SMEM)

    def far(value):
        return pltpu.with_memory_space_constraint(value, pltpu.HBM)

    flat = spectrum.reshape(bins * ROWS, LANES)
    speed = group_speed.reshape(freqs * ROWS, LANES)
    edge = pltpu.HBM((bins + freqs + 8, LANES), jnp.float32)
    messages, to_pair, to_next = pl.pallas_call(
        lambda *refs: outgoing_kernel(bins, freqs, *refs),
        out_shape=(near(LANES, LANES), edge, edge),
        in_specs=[smem] + [pl.BlockSpec(memory_space=pltpu.HBM)] * 6,
        out_specs=tuple(vmem_specs(3)),
        scratch_shapes=[
            VMEM((2, ROWS, LANES), jnp.float32),
            VMEM((2, ROWS * LANES), jnp.float32),
            VMEM((ROWS, LANES), jnp.float32),
            VMEM((bins * ROWS, LANES), jnp.float32),
            VMEM((freqs * ROWS, LANES), jnp.float32),
            VMEM((ROWS, LANES), jnp.int32),
            VMEM((2, ROWS, LANES), jnp.float32),
            pltpu.SemaphoreType.DMA((6,)),
        ],
        name="outgoing",
        compiler_params=pltpu.CompilerParams(vmem_limit_bytes=8 * MIB),
    )(
        at,
        far(ocean_current.reshape(2, ROWS, LANES)),
        far(wind_vector.reshape(2, ROWS * LANES)),
        far(ice_cover.reshape(ROWS, LANES)),
        far(flat),
        far(speed),
        far(route_slot),
    )
    pairs = [(i, i + 1) for i in range(0, blocks, 2)]
    nexts = [(i, i + 1) for i in range(1, blocks - 1, 2)]
    got = held(lax.all_to_all(messages, BLK, 0, 0, tiled=True))
    from_next = held(lax.ppermute(to_next, BLK, nexts + [(j, i) for i, j in nexts]))
    from_pair = held(lax.ppermute(to_pair, BLK, pairs + [(j, i) for i, j in pairs]))
    flat, speed = held(flat), held(speed)

    moved, parts, cell = pl.pallas_call(
        lambda *refs: move_kernel(dirs, freqs, *refs),
        out_shape=(pltpu.HBM((bins * ROWS, LANES), jnp.float32), near(bands, 48, LANES), near(48, LANES)),
        in_specs=[smem, smem] + vmem_specs(6),
        out_specs=(pl.BlockSpec(memory_space=pltpu.HBM), *vmem_specs(2)),
        scratch_shapes=[
            VMEM((LANES, LANES), jnp.float32),
            VMEM((freqs * ROWS, LANES), jnp.float32),
            VMEM((freqs * ROWS, LANES), jnp.float32),
            VMEM((freqs * ROWS, LANES), jnp.float32),
            VMEM((freqs, LANES), jnp.float32),
            VMEM((freqs, LANES), jnp.float32),
            VMEM((bins * ROWS, LANES), jnp.float32),
            VMEM((bins + freqs + 8, LANES), jnp.float32),
            VMEM((bins + freqs + 8, LANES), jnp.float32),
            pltpu.SemaphoreType.DMA((dirs,)),
        ],
        name="move",
        compiler_params=pltpu.CompilerParams(vmem_limit_bytes=8 * MIB),
    )(at, trig, got, flat, speed, from_pair, from_next, route_slot)

    parts = held(lax.all_to_all(parts, DIR, 0, 0, tiled=True))
    damping, own = pl.pallas_call(
        forcing_kernel,
        out_shape=(near(ROWS, LANES), near(LANES, LANES)),
        in_specs=[smem] + vmem_specs(1),
        out_specs=tuple(vmem_specs(2)),
        name="forcing",
        compiler_params=pltpu.CompilerParams(vmem_limit_bytes=4 * MIB),
    )(at, parts)
    ocean = held(lax.all_to_all(own, BLK, 0, 0, tiled=True))
    result = pl.pallas_call(
        lambda *refs: update_kernel(dirs, freqs, *refs),
        out_shape=f32(bins * ROWS, LANES),
        grid=(dirs,),
        in_specs=[smem, smem, pl.BlockSpec((freqs * ROWS, LANES), lambda j: (j, 0))] + vmem_specs(2),
        out_specs=pl.BlockSpec((freqs * ROWS, LANES), lambda j: (j, 0)),
        name="update",
        compiler_params=pltpu.CompilerParams(vmem_limit_bytes=4 * MIB),
        cost_estimate=pl.CostEstimate(flops=3 * bins * ROWS * LANES, bytes_accessed=8 * bins * ROWS * LANES, transcendentals=0),
    )(at, trig, pltpu.with_memory_space_constraint(moved, pltpu.HBM), cell, damping)
    ocean = pl.pallas_call(
        row_kernel,
        out_shape=f32(ROWS, LANES),
        in_specs=vmem_specs(1),
        out_specs=vmem_specs(1)[0],
        name="rows",
        compiler_params=pltpu.CompilerParams(vmem_limit_bytes=4 * MIB),
    )(ocean)
    return (result.reshape(spectrum.shape), ocean.reshape(1, 1, ROWS * LANES))


def solution(mesh):
    return jax.shard_map(
        one_step,
        mesh=mesh,
        in_specs=(
            P(DIR, None, BLK, None),
            P(None, BLK, None),
            P(None, BLK, None),
            P(BLK, None),
            P(BLK, None, None),
            P(BLK, None),
        ),
        out_specs=(P(DIR, None, BLK, None), P(DIR, BLK, None)),
        check_vma=False,
    )
```

```python
import math

import jax
import jax.numpy as jnp
import numpy as np
from jax import lax
from jax.experimental import pallas as pl
from jax.experimental.pallas import tpu as pltpu
from jax.sharding import PartitionSpec as P


BLK = "blk"
DIR = "dir"
VMEM = pltpu.VMEM
SMEM = pltpu.SMEM

COURANT = 0.15
WIND_GROWTH = 0.15
DAMP_RATE = 0.5
STEEP_COEF = 0.01
STOKES_SCALE = 0.15
RATIO_STEP = 1.1

LANES = 128
BANDS = 4
MIB = 1 << 20
UNROLL = 18
ROWS = 16
CUR_X, CUR_Y, WIND_X, WIND_Y, ICE = 0, 24, 48, 64, 80


def vmem_specs(count):
    return [pl.BlockSpec(memory_space=VMEM)] * count


def lane_of(shape):
    return lax.broadcasted_iota(jnp.int32, shape, len(shape) - 1)


def message_kernel(
    cur_hbm,
    wind_hbm,
    ice_hbm,
    out_ref,
    cur_ref,
    wind_ref,
    ice_ref,
    x_ref,
    sems,
):
    sources, targets = (cur_hbm, wind_hbm, ice_hbm), (cur_ref, wind_ref, ice_ref)
    copies = [pltpu.make_async_copy(a, b, sems.at[i]) for i, (a, b) in enumerate(zip(sources, targets))]
    for copy in copies:
        copy.start()
    for copy in copies:
        copy.wait()
    for c in range(2):
        for r in range(ROWS):
            x_ref[c, r : r + 1, :] = wind_ref[c : c + 1, LANES * r : LANES * (r + 1)]
    lane = lane_of((ROWS, LANES))

    def put(s, values, start):
        return pltpu.roll(values, (start - ROWS * s) % LANES, 1)

    for s in range(8):
        row = jnp.where(lane < CUR_Y, put(s, cur_ref[0], CUR_X + 1), put(s, cur_ref[1], CUR_Y))
        row = jnp.where(lane < WIND_X, row, put(s, x_ref[0], WIND_X))
        row = jnp.where(lane < WIND_Y, row, put(s, x_ref[1], WIND_Y))
        row = jnp.where(lane < ICE, row, put(s, ice_ref[...], ICE))
        out_ref[pl.ds(s, ROWS, stride=8), :] = row
    whole = out_ref[...]
    wide = lane_of((LANES, LANES))
    before = pltpu.roll(pltpu.roll(whole, 1, 0), LANES - ROWS, 1)
    after = pltpu.roll(pltpu.roll(whole, LANES - 1, 0), ROWS, 1)
    whole = jnp.where(wide == CUR_X, before, whole)
    out_ref[...] = jnp.where(wide == CUR_X + ROWS + 1, after, whole)


def edge_kernel(
    bins, freqs, at_ref, spec_hbm, speed_hbm, slot_hbm, pair_ref, next_ref, spec_ref, speed_ref, slot_ref, sems
):
    sources, targets = (slot_hbm, speed_hbm, spec_hbm), (slot_ref, speed_ref, spec_ref)
    copies = [pltpu.make_async_copy(a, b, sems.at[i]) for i, (a, b) in enumerate(zip(sources, targets))]
    for copy in copies:
        copy.start()
    for copy in copies:
        copy.wait()
    odd = at_ref[0] >= BANDS

    def trade(start, stop, first, last):
        pair_ref[start:stop, :] = jnp.where(odd, first, last)
        next_ref[start:stop, :] = jnp.where(odd, last, first)

    for source, start, count in ((spec_ref, 0, bins), (speed_ref, bins, freqs)):
        trade(start, start + count, source[pl.ds(0, count, stride=ROWS), :], source[pl.ds(ROWS - 1, count, stride=ROWS), :])
    sea = jnp.where(slot_ref[...] >= 0, 1.0, 0.0)
    sea = [jnp.broadcast_to(sea[r : r + 1, :], (8, LANES)) for r in (0, ROWS - 1)]
    trade(bins + freqs, bins + freqs + 8, *sea)


def move_kernel(
    dirs,
    freqs,
    at_ref,
    trig_ref,
    got_ref,
    spec_ref,
    speed_ref,
    slot_ref,
    stored_ref,
    parts_ref,
    cell_ref,
    turned_ref,
    sx_ref,
    sy_ref,
    sw_ref,
    moved_ref,
    sems,
):
    shape = (ROWS, LANES)
    row, lane = lax.broadcasted_iota(jnp.int32, shape, 0), lane_of(shape)
    turned_ref[...] = got_ref[...].T

    def shifted_down(values):
        return pltpu.roll(values, 1, 0)

    def next_y(values):
        return pltpu.roll(values, LANES - 1, 1)

    slots = slot_ref[...]
    sea = jnp.where(slots >= 0, 1.0, 0.0)
    half = 0.5 * COURANT
    open_x = jnp.where(row > 0, half * sea * shifted_down(sea), 0.0)
    open_y = jnp.where(lane < LANES - 1, half * sea * next_y(sea), 0.0)
    flow_x = open_x * (turned_ref[CUR_X : CUR_X + ROWS, :] + turned_ref[CUR_X + 1 : CUR_X + ROWS + 1, :])
    cur_y = turned_ref[CUR_Y : CUR_Y + ROWS, :]
    flow_y = open_y * (cur_y + next_y(cur_y))
    flow_w = pltpu.roll(flow_y, 1, 1)

    owner, place = jnp.maximum(slots, 0) // 16, jnp.where(slots >= 0, slots % 16, -1)
    wind_x, wind_y, ice = (jnp.zeros(shape, jnp.float32) for _ in range(3))
    for s in range(16):
        here = place == s

        def picked(start, old):
            table = jnp.broadcast_to(turned_ref[start + s : start + s + 1, :], shape)
            return jnp.where(here, jnp.take_along_axis(table, owner, axis=1), old)

        wind_x, wind_y, ice = picked(WIND_X, wind_x), picked(WIND_Y, wind_y), picked(ICE, ice)
    gain = WIND_GROWTH * (1.0 - ice)
    cell_ref[0:16, :] = wind_x
    cell_ref[16:32, :] = wind_y
    cell_ref[32:48, :] = gain
    for side, x in enumerate((CUR_X, CUR_X + ROWS)):
        cell_ref[48 + side : 49 + side, :] = turned_ref[x : x + 1, :] + turned_ref[x + 1 : x + 2, :]

    def faces(k, _):
        base = pl.multiple_of(k * ROWS, ROWS)
        speed = speed_ref[pl.ds(base, ROWS), :]
        sx_ref[pl.ds(base, ROWS), :] = open_x * (speed + shifted_down(speed))
        side = open_y * (speed + next_y(speed))
        sy_ref[pl.ds(base, ROWS), :] = side
        sw_ref[pl.ds(base, ROWS), :] = pltpu.roll(side, 1, 1)
        return 0

    lax.fori_loop(0, freqs, faces, 0, unroll=12)

    zero = jnp.zeros(shape, jnp.float32)
    moment, stress_x, stress_y, drift_x, drift_y, damp_x, damp_y = (zero,) * 7
    at = at_ref[0] % BANDS
    copies = []
    for j in range(dirs):
        cosine, sine = trig_ref[at, j], trig_ref[at, dirs + j]

        def step(k, sums):
            second, third, fourth = sums
            base = pl.multiple_of(k * ROWS, ROWS)
            here = pl.multiple_of(j * freqs * ROWS + k * ROWS, ROWS)
            energy = spec_ref[pl.ds(here, ROWS), :]
            u = sx_ref[pl.ds(base, ROWS), :] * cosine + flow_x
            below = u * jnp.where(u > 0.0, shifted_down(energy), energy)
            above = pltpu.roll(below, ROWS - 1, 0)
            v = sy_ref[pl.ds(base, ROWS), :] * sine + flow_y
            right = v * jnp.where(v > 0.0, energy, next_y(energy))
            w = sw_ref[pl.ds(base, ROWS), :] * sine + flow_w
            left = w * jnp.where(w > 0.0, pltpu.roll(energy, 1, 1), energy)
            moved = sea * (energy - ((above - below) + (right - left)))
            moved_ref[pl.ds(here, ROWS), :] = moved
            return (
                second * (RATIO_STEP**-2) + moved,
                third * (RATIO_STEP**-3) + moved,
                fourth * (RATIO_STEP**-4) + moved,
            )

        def out_copy():
            part = pl.ds(j * freqs * ROWS, freqs * ROWS)
            return pltpu.make_async_copy(moved_ref.at[part, :], stored_ref.at[part, :], sems.at[j])

        second, third, fourth = lax.fori_loop(0, freqs, step, (zero, zero, zero), unroll=UNROLL)
        copies.append(out_copy())
        copies[-1].start()
        wind_gain = gain * jnp.maximum(wind_x * cosine + wind_y * sine, 0.0)
        push = wind_gain * second
        drift = third + wind_gain * fourth
        moment += second
        stress_x += cosine * push
        stress_y += sine * push
        drift_x += cosine * drift
        drift_y += sine * drift
        damp_x += cosine * fourth
        damp_y += sine * fourth
    for c, (main, damped) in enumerate(((stress_x, zero), (stress_y, zero), (drift_x, damp_x), (drift_y, damp_y))):
        parts_ref[c, 0:16, :] = moment
        parts_ref[c, 16:32, :] = main
        parts_ref[c, 32:48, :] = damped
    for copy in copies:
        copy.wait()


def fix_kernel(
    dirs,
    freqs,
    at_ref,
    trig_ref,
    cell_ref,
    from_pair_ref,
    from_next_ref,
    to_pair_ref,
    to_next_ref,
    parts_ref,
    out_ref,
    fix_ref,
    behind_ref,
    ahead_ref,
):
    bins = dirs * freqs
    odd, at = at_ref[0] >= BANDS, at_ref[0] % BANDS
    power = lax.broadcasted_iota(jnp.int32, (freqs, LANES), 0).astype(jnp.float32) - (freqs - 1)
    weights = [jnp.exp(power * (p * math.log(RATIO_STEP))) for p in (2, 3, 4)]
    out_ref[...] = parts_ref[...]
    faces = (
        (0, 1.0, from_pair_ref, from_next_ref, to_pair_ref, to_next_ref),
        (ROWS - 1, -1.0, to_next_ref, to_pair_ref, from_next_ref, from_pair_ref),
    )
    for side, (row, sign, behind_odd, behind_even, ahead_odd, ahead_even) in enumerate(faces):
        behind_ref[...] = jnp.where(odd, behind_odd[...], behind_even[...])
        ahead_ref[...] = jnp.where(odd, ahead_odd[...], ahead_even[...])
        mask = slice(bins + freqs, bins + freqs + 1)
        opened = (sign * 0.5 * COURANT) * behind_ref[mask, :] * ahead_ref[mask, :]
        flow = opened * cell_ref[48 + side : 49 + side, :]
        speed = opened * (behind_ref[bins : bins + freqs, :] + ahead_ref[bins : bins + freqs, :])
        wind_x, wind_y, gain = (cell_ref[r : r + 1, :] for r in (row, 16 + row, 32 + row))
        moment, stress_x, stress_y, drift_x, drift_y, damp_x, damp_y = (jnp.zeros((1, LANES), jnp.float32),) * 7
        for j in range(dirs):
            cosine, sine = trig_ref[at, j], trig_ref[at, dirs + j]
            u = speed * cosine + flow
            part = slice(j * freqs, (j + 1) * freqs)
            flux = u * jnp.where(sign * u > 0.0, behind_ref[part, :], ahead_ref[part, :])
            fix_ref[side, part, :] = flux
            second, third, fourth = (jnp.sum(w * flux, axis=0, keepdims=True) for w in weights)
            wind_gain = gain * jnp.maximum(wind_x * cosine + wind_y * sine, 0.0)
            push = wind_gain * second
            drift = third + wind_gain * fourth
            moment += second
            stress_x += cosine * push
            stress_y += sine * push
            drift_x += cosine * drift
            drift_y += sine * drift
            damp_x += cosine * fourth
            damp_y += sine * fourth
        for c, (main, damped) in enumerate(((stress_x, None), (stress_y, None), (drift_x, damp_x), (drift_y, damp_y))):
            out_ref[c, row : row + 1, :] += moment
            out_ref[c, 16 + row : 17 + row, :] += main
            if damped is not None:
                out_ref[c, 32 + row : 33 + row, :] += damped


def forcing_kernel(at_ref, parts_ref, damping_ref, out_ref):
    parts = (parts_ref[0] + parts_ref[1]) + (parts_ref[2] + parts_ref[3])
    steepness = STEEP_COEF * parts[0:16]
    damping = DAMP_RATE * steepness / (1.0 + steepness)
    damping_ref[...] = damping
    own = parts[16:32] - damping * parts[32:48]
    own = jnp.where(at_ref[0] % BANDS < 2, 1.0, STOKES_SCALE) * own
    out_ref[...] = jnp.concatenate([own, jnp.zeros((LANES - ROWS, LANES), jnp.float32)], axis=0).T


def update_kernel(dirs, freqs, at_ref, trig_ref, moved_ref, cell_ref, damping_ref, fix_ref, out_ref):
    j, at = pl.program_id(0), at_ref[0] % BANDS
    cosine, sine = trig_ref[at, j], trig_ref[at, dirs + j]
    wind = jnp.maximum(cell_ref[0:16, :] * cosine + cell_ref[16:32, :] * sine, 0.0)
    growth = cell_ref[32:48, :] * wind - damping_ref[...]
    row = lax.broadcasted_iota(jnp.int32, (ROWS, LANES), 0)
    for k in range(freqs):
        ratio = RATIO_STEP ** (k - freqs + 1)
        first, last = (jnp.broadcast_to(fix_ref[side, pl.ds(j * freqs + k, 1), :], (ROWS, LANES)) for side in (0, 1))
        edge = jnp.where(row == 0, first, jnp.where(row == ROWS - 1, last, 0.0))
        moved = moved_ref[k * ROWS : (k + 1) * ROWS, :] + edge
        out_ref[k * ROWS : (k + 1) * ROWS, :] = moved * (1.0 + ratio * growth)


def row_kernel(got_ref, out_ref):
    lane = lane_of((ROWS, LANES))
    row = got_ref[pl.ds(0, ROWS, stride=8), :]
    for s in range(1, 8):
        row = jnp.where(lane < ROWS * s, row, pltpu.roll(got_ref[pl.ds(s, ROWS, stride=8), :], ROWS * s, 1))
    out_ref[...] = row


def f32(*shape):
    return jax.ShapeDtypeStruct(shape, jnp.float32)


def near(*shape):
    return VMEM(shape, jnp.float32)


def held(value):
    return pltpu.with_memory_space_constraint(value, VMEM)


def one_step(spectrum, group_speed, ocean_current, route_slot, wind_vector, ice_cover):
    dirs, freqs, _, _ = spectrum.shape
    bands, blocks = lax.axis_size(DIR), lax.axis_size(BLK)
    bins = dirs * freqs
    at = (lax.axis_index(DIR) + bands * (lax.axis_index(BLK) & 1)).astype(jnp.int32).reshape(1)
    angles = (2.0 * np.pi * np.arange(bands * dirs, dtype=np.float32) / np.float32(bands * dirs)).astype(np.float32)
    angles = angles.astype(np.float64).reshape(bands, dirs)
    trig = jnp.asarray(np.concatenate([np.cos(angles), np.sin(angles)], axis=1).astype(np.float32))
    smem = pl.BlockSpec(memory_space=SMEM)

    def far(value):
        return pltpu.with_memory_space_constraint(value, pltpu.HBM)

    messages = pl.pallas_call(
        message_kernel,
        out_shape=near(LANES, LANES),
        in_specs=[pl.BlockSpec(memory_space=pltpu.HBM)] * 3,
        out_specs=vmem_specs(1)[0],
        scratch_shapes=[
            VMEM((2, ROWS, LANES), jnp.float32),
            VMEM((2, ROWS * LANES), jnp.float32),
            VMEM((ROWS, LANES), jnp.float32),
            VMEM((2, ROWS, LANES), jnp.float32),
            pltpu.SemaphoreType.DMA((3,)),
        ],
        name="messages",
        compiler_params=pltpu.CompilerParams(vmem_limit_bytes=4 * MIB),
    )(
        far(ocean_current.reshape(2, ROWS, LANES)),
        far(wind_vector.reshape(2, ROWS * LANES)),
        far(ice_cover.reshape(ROWS, LANES)),
    )
    flat, speed = spectrum.reshape(bins * ROWS, LANES), group_speed.reshape(freqs * ROWS, LANES)
    edge = near(bins + freqs + 8, LANES)
    edges = pl.pallas_call(
        lambda *refs: edge_kernel(bins, freqs, *refs),
        out_shape=(edge, edge),
        in_specs=[smem] + [pl.BlockSpec(memory_space=pltpu.HBM)] * 3,
        out_specs=tuple(vmem_specs(2)),
        scratch_shapes=[
            VMEM((bins * ROWS, LANES), jnp.float32),
            VMEM((freqs * ROWS, LANES), jnp.float32),
            VMEM((ROWS, LANES), jnp.int32),
            pltpu.SemaphoreType.DMA((3,)),
        ],
        name="edges",
        compiler_params=pltpu.CompilerParams(vmem_limit_bytes=8 * MIB),
    )
    to_pair, to_next = edges(at, far(flat), far(speed), far(route_slot))
    flat, speed = held(flat), held(speed)
    pairs = [(i, i + 1) for i in range(0, blocks, 2)]
    nexts = [(i, i + 1) for i in range(1, blocks - 1, 2)]
    got = held(lax.all_to_all(messages, BLK, 0, 0, tiled=True))
    from_next = held(lax.ppermute(to_next, BLK, nexts + [(j, i) for i, j in nexts]))
    from_pair = held(lax.ppermute(to_pair, BLK, pairs + [(j, i) for i, j in pairs]))
    move = pl.pallas_call(
        lambda *refs: move_kernel(dirs, freqs, *refs),
        out_shape=(pltpu.HBM((bins * ROWS, LANES), jnp.float32), near(bands, 48, LANES), near(56, LANES)),
        in_specs=[smem, smem] + vmem_specs(4),
        out_specs=(pl.BlockSpec(memory_space=pltpu.HBM), *vmem_specs(2)),
        scratch_shapes=[
            VMEM((LANES, LANES), jnp.float32),
            VMEM((freqs * ROWS, LANES), jnp.float32),
            VMEM((freqs * ROWS, LANES), jnp.float32),
            VMEM((freqs * ROWS, LANES), jnp.float32),
            VMEM((bins * ROWS, LANES), jnp.float32),
            pltpu.SemaphoreType.DMA((dirs,)),
        ],
        name="move",
        compiler_params=pltpu.CompilerParams(vmem_limit_bytes=8 * MIB),
    )
    moved, parts, cell = move(at, trig, got, flat, speed, route_slot)
    parts, fixes = pl.pallas_call(
        lambda *refs: fix_kernel(dirs, freqs, *refs),
        out_shape=(near(bands, 48, LANES), near(2, bins, LANES)),
        in_specs=[smem, smem] + vmem_specs(6),
        out_specs=tuple(vmem_specs(2)),
        scratch_shapes=[VMEM((bins + freqs + 8, LANES), jnp.float32), VMEM((bins + freqs + 8, LANES), jnp.float32)],
        name="fix",
        compiler_params=pltpu.CompilerParams(vmem_limit_bytes=4 * MIB),
    )(at, trig, cell, from_pair, from_next, to_pair, to_next, parts)

    parts = held(lax.all_to_all(parts, DIR, 0, 0, tiled=True))
    damping, own = pl.pallas_call(
        forcing_kernel,
        out_shape=(near(ROWS, LANES), near(LANES, LANES)),
        in_specs=[smem] + vmem_specs(1),
        out_specs=tuple(vmem_specs(2)),
        name="forcing",
        compiler_params=pltpu.CompilerParams(vmem_limit_bytes=4 * MIB),
    )(at, parts)
    ocean = held(lax.all_to_all(own, BLK, 0, 0, tiled=True))
    result = pl.pallas_call(
        lambda *refs: update_kernel(dirs, freqs, *refs),
        out_shape=f32(bins * ROWS, LANES),
        grid=(dirs,),
        in_specs=[smem, smem, pl.BlockSpec((freqs * ROWS, LANES), lambda j: (j, 0))] + vmem_specs(3),
        out_specs=pl.BlockSpec((freqs * ROWS, LANES), lambda j: (j, 0)),
        name="update",
        compiler_params=pltpu.CompilerParams(vmem_limit_bytes=4 * MIB),
        cost_estimate=pl.CostEstimate(flops=3 * bins * ROWS * LANES, bytes_accessed=8 * bins * ROWS * LANES, transcendentals=0),
    )(at, trig, pltpu.with_memory_space_constraint(moved, pltpu.HBM), cell, damping, fixes)
    ocean = pl.pallas_call(
        row_kernel,
        out_shape=f32(ROWS, LANES),
        in_specs=vmem_specs(1),
        out_specs=vmem_specs(1)[0],
        name="rows",
        compiler_params=pltpu.CompilerParams(vmem_limit_bytes=4 * MIB),
    )(ocean)
    return (result.reshape(spectrum.shape), ocean.reshape(1, 1, ROWS * LANES))


def solution(mesh):
    return jax.shard_map(
        one_step,
        mesh=mesh,
        in_specs=(
            P(DIR, None, BLK, None),
            P(None, BLK, None),
            P(None, BLK, None),
            P(BLK, None),
            P(BLK, None, None),
            P(BLK, None),
        ),
        out_specs=(P(DIR, None, BLK, None), P(DIR, BLK, None)),
        check_vma=False,
    )
```

```python
import math

import jax
import jax.numpy as jnp
import numpy as np
from jax import lax
from jax.experimental import pallas as pl
from jax.experimental.pallas import tpu as pltpu
from jax.sharding import PartitionSpec as P


BLK = "blk"
DIR = "dir"
VMEM = pltpu.VMEM
SMEM = pltpu.SMEM

COURANT = 0.15
WIND_GROWTH = 0.15
DAMP_RATE = 0.5
STEEP_COEF = 0.01
STOKES_SCALE = 0.15
RATIO_STEP = 1.1

LANES = 128
BANDS = 4
MIB = 1 << 20
UNROLL = 18
ROWS = 16
CUR_X, CUR_Y, WIND_X, WIND_Y, ICE = 0, 24, 48, 64, 80


def vmem_specs(count):
    return [pl.BlockSpec(memory_space=VMEM)] * count


def lane_of(shape):
    return lax.broadcasted_iota(jnp.int32, shape, len(shape) - 1)


def outgoing_kernel(
    bins,
    freqs,
    at_ref,
    cur_hbm,
    wind_hbm,
    ice_hbm,
    spec_hbm,
    speed_hbm,
    slot_hbm,
    out_ref,
    pair_ref,
    next_ref,
    cur_ref,
    wind_ref,
    ice_ref,
    spec_ref,
    speed_ref,
    slot_ref,
    x_ref,
    sems,
):
    sources = (cur_hbm, wind_hbm, ice_hbm, slot_hbm, speed_hbm, spec_hbm)
    targets = (cur_ref, wind_ref, ice_ref, slot_ref, speed_ref, spec_ref)
    copies = [pltpu.make_async_copy(a, b, sems.at[i]) for i, (a, b) in enumerate(zip(sources, targets))]
    for copy in copies:
        copy.start()
    for copy in copies[:3]:
        copy.wait()
    for c in range(2):
        for r in range(ROWS):
            x_ref[c, r : r + 1, :] = wind_ref[c : c + 1, LANES * r : LANES * (r + 1)]
    lane = lane_of((ROWS, LANES))

    def put(s, values, start):
        return pltpu.roll(values, (start - ROWS * s) % LANES, 1)

    for s in range(8):
        row = jnp.where(lane < CUR_Y, put(s, cur_ref[0], CUR_X + 1), put(s, cur_ref[1], CUR_Y))
        row = jnp.where(lane < WIND_X, row, put(s, x_ref[0], WIND_X))
        row = jnp.where(lane < WIND_Y, row, put(s, x_ref[1], WIND_Y))
        row = jnp.where(lane < ICE, row, put(s, ice_ref[...], ICE))
        out_ref[pl.ds(s, ROWS, stride=8), :] = row
    whole = out_ref[...]
    wide = lane_of((LANES, LANES))
    before = pltpu.roll(pltpu.roll(whole, 1, 0), LANES - ROWS, 1)
    after = pltpu.roll(pltpu.roll(whole, LANES - 1, 0), ROWS, 1)
    whole = jnp.where(wide == CUR_X, before, whole)
    out_ref[...] = jnp.where(wide == CUR_X + ROWS + 1, after, whole)
    odd = at_ref[0] >= BANDS
    for copy in copies[3:]:
        copy.wait()

    def trade(start, stop, first, last):
        pair_ref[start:stop, :] = jnp.where(odd, first, last)
        next_ref[start:stop, :] = jnp.where(odd, last, first)

    for source, start, count in ((spec_ref, 0, bins), (speed_ref, bins, freqs)):
        trade(start, start + count, source[pl.ds(0, count, stride=ROWS), :], source[pl.ds(ROWS - 1, count, stride=ROWS), :])
    sea = jnp.where(slot_ref[...] >= 0, 1.0, 0.0)
    sea = [jnp.broadcast_to(sea[r : r + 1, :], (8, LANES)) for r in (0, ROWS - 1)]
    trade(bins + freqs, bins + freqs + 8, *sea)


def move_kernel(
    dirs,
    freqs,
    at_ref,
    trig_ref,
    got_ref,
    spec_ref,
    speed_ref,
    slot_ref,
    stored_ref,
    parts_ref,
    cell_ref,
    turned_ref,
    sx_ref,
    sy_ref,
    sw_ref,
    moved_ref,
    sems,
):
    shape = (ROWS, LANES)
    row, lane = lax.broadcasted_iota(jnp.int32, shape, 0), lane_of(shape)
    turned_ref[...] = got_ref[...].T

    def shifted_down(values):
        return pltpu.roll(values, 1, 0)

    def next_y(values):
        return pltpu.roll(values, LANES - 1, 1)

    slots = slot_ref[...]
    sea = jnp.where(slots >= 0, 1.0, 0.0)
    half = 0.5 * COURANT
    open_x = jnp.where(row > 0, half * sea * shifted_down(sea), 0.0)
    open_y = jnp.where(lane < LANES - 1, half * sea * next_y(sea), 0.0)
    flow_x = open_x * (turned_ref[CUR_X : CUR_X + ROWS, :] + turned_ref[CUR_X + 1 : CUR_X + ROWS + 1, :])
    cur_y = turned_ref[CUR_Y : CUR_Y + ROWS, :]
    flow_y = open_y * (cur_y + next_y(cur_y))
    flow_w = pltpu.roll(flow_y, 1, 1)

    owner, place = jnp.maximum(slots, 0) // 16, jnp.where(slots >= 0, slots % 16, -1)
    wind_x, wind_y, ice = (jnp.zeros(shape, jnp.float32) for _ in range(3))
    for s in range(16):
        here = place == s

        def picked(start, old):
            table = jnp.broadcast_to(turned_ref[start + s : start + s + 1, :], shape)
            return jnp.where(here, jnp.take_along_axis(table, owner, axis=1), old)

        wind_x, wind_y, ice = picked(WIND_X, wind_x), picked(WIND_Y, wind_y), picked(ICE, ice)
    gain = WIND_GROWTH * (1.0 - ice)
    cell_ref[0:16, :] = wind_x
    cell_ref[16:32, :] = wind_y
    cell_ref[32:48, :] = gain
    for side, x in enumerate((CUR_X, CUR_X + ROWS)):
        cell_ref[48 + side : 49 + side, :] = turned_ref[x : x + 1, :] + turned_ref[x + 1 : x + 2, :]

    def faces(k, _):
        base = pl.multiple_of(k * ROWS, ROWS)
        speed = speed_ref[pl.ds(base, ROWS), :]
        sx_ref[pl.ds(base, ROWS), :] = open_x * (speed + shifted_down(speed))
        side = open_y * (speed + next_y(speed))
        sy_ref[pl.ds(base, ROWS), :] = side
        sw_ref[pl.ds(base, ROWS), :] = pltpu.roll(side, 1, 1)
        return 0

    lax.fori_loop(0, freqs, faces, 0, unroll=12)

    zero = jnp.zeros(shape, jnp.float32)
    moment, stress_x, stress_y, drift_x, drift_y, damp_x, damp_y = (zero,) * 7
    at = at_ref[0] % BANDS
    copies = []
    for j in range(dirs):
        cosine, sine = trig_ref[at, j], trig_ref[at, dirs + j]

        def step(k, sums):
            second, third, fourth = sums
            base = pl.multiple_of(k * ROWS, ROWS)
            here = pl.multiple_of(j * freqs * ROWS + k * ROWS, ROWS)
            energy = spec_ref[pl.ds(here, ROWS), :]
            u = sx_ref[pl.ds(base, ROWS), :] * cosine + flow_x
            below = u * jnp.where(u > 0.0, shifted_down(energy), energy)
            above = pltpu.roll(below, ROWS - 1, 0)
            v = sy_ref[pl.ds(base, ROWS), :] * sine + flow_y
            right = v * jnp.where(v > 0.0, energy, next_y(energy))
            w = sw_ref[pl.ds(base, ROWS), :] * sine + flow_w
            left = w * jnp.where(w > 0.0, pltpu.roll(energy, 1, 1), energy)
            moved = sea * (energy - ((above - below) + (right - left)))
            moved_ref[pl.ds(here, ROWS), :] = moved
            return (
                second * (RATIO_STEP**-2) + moved,
                third * (RATIO_STEP**-3) + moved,
                fourth * (RATIO_STEP**-4) + moved,
            )

        def out_copy():
            part = pl.ds(j * freqs * ROWS, freqs * ROWS)
            return pltpu.make_async_copy(moved_ref.at[part, :], stored_ref.at[part, :], sems.at[j])

        second, third, fourth = lax.fori_loop(0, freqs, step, (zero, zero, zero), unroll=UNROLL)
        copies.append(out_copy())
        copies[-1].start()
        wind_gain = gain * jnp.maximum(wind_x * cosine + wind_y * sine, 0.0)
        push = wind_gain * second
        drift = third + wind_gain * fourth
        moment += second
        stress_x += cosine * push
        stress_y += sine * push
        drift_x += cosine * drift
        drift_y += sine * drift
        damp_x += cosine * fourth
        damp_y += sine * fourth
    for c, (main, damped) in enumerate(((stress_x, zero), (stress_y, zero), (drift_x, damp_x), (drift_y, damp_y))):
        parts_ref[c, 0:16, :] = moment
        parts_ref[c, 16:32, :] = main
        parts_ref[c, 32:48, :] = damped
    for copy in copies:
        copy.wait()


def fix_kernel(
    dirs,
    freqs,
    at_ref,
    trig_ref,
    cell_ref,
    from_pair_ref,
    from_next_ref,
    to_pair_ref,
    to_next_ref,
    parts_ref,
    out_ref,
    fix_ref,
    behind_ref,
    ahead_ref,
):
    bins = dirs * freqs
    odd, at = at_ref[0] >= BANDS, at_ref[0] % BANDS
    power = lax.broadcasted_iota(jnp.int32, (freqs, LANES), 0).astype(jnp.float32) - (freqs - 1)
    weights = [jnp.exp(power * (p * math.log(RATIO_STEP))) for p in (2, 3, 4)]
    out_ref[...] = parts_ref[...]
    faces = (
        (0, 1.0, from_pair_ref, from_next_ref, to_pair_ref, to_next_ref),
        (ROWS - 1, -1.0, to_next_ref, to_pair_ref, from_next_ref, from_pair_ref),
    )
    for side, (row, sign, behind_odd, behind_even, ahead_odd, ahead_even) in enumerate(faces):
        behind_ref[...] = jnp.where(odd, behind_odd[...], behind_even[...])
        ahead_ref[...] = jnp.where(odd, ahead_odd[...], ahead_even[...])
        mask = slice(bins + freqs, bins + freqs + 1)
        opened = (sign * 0.5 * COURANT) * behind_ref[mask, :] * ahead_ref[mask, :]
        flow = opened * cell_ref[48 + side : 49 + side, :]
        speed = opened * (behind_ref[bins : bins + freqs, :] + ahead_ref[bins : bins + freqs, :])
        wind_x, wind_y, gain = (cell_ref[r : r + 1, :] for r in (row, 16 + row, 32 + row))
        moment, stress_x, stress_y, drift_x, drift_y, damp_x, damp_y = (jnp.zeros((1, LANES), jnp.float32),) * 7
        for j in range(dirs):
            cosine, sine = trig_ref[at, j], trig_ref[at, dirs + j]
            u = speed * cosine + flow
            part = slice(j * freqs, (j + 1) * freqs)
            flux = u * jnp.where(sign * u > 0.0, behind_ref[part, :], ahead_ref[part, :])
            fix_ref[side, part, :] = flux
            second, third, fourth = (jnp.sum(w * flux, axis=0, keepdims=True) for w in weights)
            wind_gain = gain * jnp.maximum(wind_x * cosine + wind_y * sine, 0.0)
            push = wind_gain * second
            drift = third + wind_gain * fourth
            moment += second
            stress_x += cosine * push
            stress_y += sine * push
            drift_x += cosine * drift
            drift_y += sine * drift
            damp_x += cosine * fourth
            damp_y += sine * fourth
        for c, (main, damped) in enumerate(((stress_x, None), (stress_y, None), (drift_x, damp_x), (drift_y, damp_y))):
            out_ref[c, row : row + 1, :] += moment
            out_ref[c, 16 + row : 17 + row, :] += main
            if damped is not None:
                out_ref[c, 32 + row : 33 + row, :] += damped


def forcing_kernel(at_ref, parts_ref, damping_ref, out_ref):
    parts = (parts_ref[0] + parts_ref[1]) + (parts_ref[2] + parts_ref[3])
    steepness = STEEP_COEF * parts[0:16]
    damping = DAMP_RATE * steepness / (1.0 + steepness)
    damping_ref[...] = damping
    own = parts[16:32] - damping * parts[32:48]
    own = jnp.where(at_ref[0] % BANDS < 2, 1.0, STOKES_SCALE) * own
    out_ref[...] = jnp.concatenate([own, jnp.zeros((LANES - ROWS, LANES), jnp.float32)], axis=0).T


def update_kernel(dirs, freqs, at_ref, trig_ref, moved_ref, cell_ref, damping_ref, fix_ref, out_ref):
    j, at = pl.program_id(0), at_ref[0] % BANDS
    cosine, sine = trig_ref[at, j], trig_ref[at, dirs + j]
    wind = jnp.maximum(cell_ref[0:16, :] * cosine + cell_ref[16:32, :] * sine, 0.0)
    growth = cell_ref[32:48, :] * wind - damping_ref[...]
    row = lax.broadcasted_iota(jnp.int32, (ROWS, LANES), 0)
    for k in range(freqs):
        ratio = RATIO_STEP ** (k - freqs + 1)
        first, last = (jnp.broadcast_to(fix_ref[side, pl.ds(j * freqs + k, 1), :], (ROWS, LANES)) for side in (0, 1))
        edge = jnp.where(row == 0, first, jnp.where(row == ROWS - 1, last, 0.0))
        moved = moved_ref[k * ROWS : (k + 1) * ROWS, :] + edge
        out_ref[k * ROWS : (k + 1) * ROWS, :] = moved * (1.0 + ratio * growth)


def row_kernel(got_ref, out_ref):
    lane = lane_of((ROWS, LANES))
    row = got_ref[pl.ds(0, ROWS, stride=8), :]
    for s in range(1, 8):
        row = jnp.where(lane < ROWS * s, row, pltpu.roll(got_ref[pl.ds(s, ROWS, stride=8), :], ROWS * s, 1))
    out_ref[...] = row


def f32(*shape):
    return jax.ShapeDtypeStruct(shape, jnp.float32)


def near(*shape):
    return VMEM(shape, jnp.float32)


def held(value):
    return pltpu.with_memory_space_constraint(value, VMEM)


def one_step(spectrum, group_speed, ocean_current, route_slot, wind_vector, ice_cover):
    dirs, freqs, _, _ = spectrum.shape
    bands, blocks = lax.axis_size(DIR), lax.axis_size(BLK)
    bins = dirs * freqs
    at = (lax.axis_index(DIR) + bands * (lax.axis_index(BLK) & 1)).astype(jnp.int32).reshape(1)
    angles = (2.0 * np.pi * np.arange(bands * dirs, dtype=np.float32) / np.float32(bands * dirs)).astype(np.float32)
    angles = angles.astype(np.float64).reshape(bands, dirs)
    trig = jnp.asarray(np.concatenate([np.cos(angles), np.sin(angles)], axis=1).astype(np.float32))
    smem = pl.BlockSpec(memory_space=SMEM)

    def far(value):
        return pltpu.with_memory_space_constraint(value, pltpu.HBM)

    flat, speed = spectrum.reshape(bins * ROWS, LANES), group_speed.reshape(freqs * ROWS, LANES)
    edge = near(bins + freqs + 8, LANES)
    messages, to_pair, to_next = pl.pallas_call(
        lambda *refs: outgoing_kernel(bins, freqs, *refs),
        out_shape=(near(LANES, LANES), edge, edge),
        in_specs=[smem] + [pl.BlockSpec(memory_space=pltpu.HBM)] * 6,
        out_specs=tuple(vmem_specs(3)),
        scratch_shapes=[
            VMEM((2, ROWS, LANES), jnp.float32),
            VMEM((2, ROWS * LANES), jnp.float32),
            VMEM((ROWS, LANES), jnp.float32),
            VMEM((bins * ROWS, LANES), jnp.float32),
            VMEM((freqs * ROWS, LANES), jnp.float32),
            VMEM((ROWS, LANES), jnp.int32),
            VMEM((2, ROWS, LANES), jnp.float32),
            pltpu.SemaphoreType.DMA((6,)),
        ],
        name="outgoing",
        compiler_params=pltpu.CompilerParams(vmem_limit_bytes=8 * MIB),
    )(
        at,
        far(ocean_current.reshape(2, ROWS, LANES)),
        far(wind_vector.reshape(2, ROWS * LANES)),
        far(ice_cover.reshape(ROWS, LANES)),
        far(flat),
        far(speed),
        far(route_slot),
    )
    flat, speed = held(flat), held(speed)
    pairs = [(i, i + 1) for i in range(0, blocks, 2)]
    nexts = [(i, i + 1) for i in range(1, blocks - 1, 2)]
    got = held(lax.all_to_all(messages, BLK, 0, 0, tiled=True))
    from_next = held(lax.ppermute(to_next, BLK, nexts + [(j, i) for i, j in nexts]))
    from_pair = held(lax.ppermute(to_pair, BLK, pairs + [(j, i) for i, j in pairs]))
    move = pl.pallas_call(
        lambda *refs: move_kernel(dirs, freqs, *refs),
        out_shape=(pltpu.HBM((bins * ROWS, LANES), jnp.float32), near(bands, 48, LANES), near(56, LANES)),
        in_specs=[smem, smem] + vmem_specs(4),
        out_specs=(pl.BlockSpec(memory_space=pltpu.HBM), *vmem_specs(2)),
        scratch_shapes=[
            VMEM((LANES, LANES), jnp.float32),
            VMEM((freqs * ROWS, LANES), jnp.float32),
            VMEM((freqs * ROWS, LANES), jnp.float32),
            VMEM((freqs * ROWS, LANES), jnp.float32),
            VMEM((bins * ROWS, LANES), jnp.float32),
            pltpu.SemaphoreType.DMA((dirs,)),
        ],
        name="move",
        compiler_params=pltpu.CompilerParams(vmem_limit_bytes=8 * MIB),
    )
    moved, parts, cell = move(at, trig, got, flat, speed, route_slot)
    parts, fixes = pl.pallas_call(
        lambda *refs: fix_kernel(dirs, freqs, *refs),
        out_shape=(near(bands, 48, LANES), near(2, bins, LANES)),
        in_specs=[smem, smem] + vmem_specs(6),
        out_specs=tuple(vmem_specs(2)),
        scratch_shapes=[VMEM((bins + freqs + 8, LANES), jnp.float32), VMEM((bins + freqs + 8, LANES), jnp.float32)],
        name="fix",
        compiler_params=pltpu.CompilerParams(vmem_limit_bytes=4 * MIB),
    )(at, trig, cell, from_pair, from_next, to_pair, to_next, parts)

    parts = held(lax.all_to_all(parts, DIR, 0, 0, tiled=True))
    damping, own = pl.pallas_call(
        forcing_kernel,
        out_shape=(near(ROWS, LANES), near(LANES, LANES)),
        in_specs=[smem] + vmem_specs(1),
        out_specs=tuple(vmem_specs(2)),
        name="forcing",
        compiler_params=pltpu.CompilerParams(vmem_limit_bytes=4 * MIB),
    )(at, parts)
    ocean = held(lax.all_to_all(own, BLK, 0, 0, tiled=True))
    result = pl.pallas_call(
        lambda *refs: update_kernel(dirs, freqs, *refs),
        out_shape=f32(bins * ROWS, LANES),
        grid=(dirs,),
        in_specs=[smem, smem, pl.BlockSpec((freqs * ROWS, LANES), lambda j: (j, 0))] + vmem_specs(3),
        out_specs=pl.BlockSpec((freqs * ROWS, LANES), lambda j: (j, 0)),
        name="update",
        compiler_params=pltpu.CompilerParams(vmem_limit_bytes=4 * MIB),
        cost_estimate=pl.CostEstimate(flops=3 * bins * ROWS * LANES, bytes_accessed=8 * bins * ROWS * LANES, transcendentals=0),
    )(at, trig, pltpu.with_memory_space_constraint(moved, pltpu.HBM), cell, damping, fixes)
    ocean = pl.pallas_call(
        row_kernel,
        out_shape=f32(ROWS, LANES),
        in_specs=vmem_specs(1),
        out_specs=vmem_specs(1)[0],
        name="rows",
        compiler_params=pltpu.CompilerParams(vmem_limit_bytes=4 * MIB),
    )(ocean)
    return (result.reshape(spectrum.shape), ocean.reshape(1, 1, ROWS * LANES))


def solution(mesh):
    return jax.shard_map(
        one_step,
        mesh=mesh,
        in_specs=(
            P(DIR, None, BLK, None),
            P(None, BLK, None),
            P(None, BLK, None),
            P(BLK, None),
            P(BLK, None, None),
            P(BLK, None),
        ),
        out_specs=(P(DIR, None, BLK, None), P(DIR, BLK, None)),
        check_vma=False,
    )
```

```python
import math

import jax
import jax.numpy as jnp
import numpy as np
from jax import lax
from jax.experimental import pallas as pl
from jax.experimental.pallas import tpu as pltpu
from jax.sharding import PartitionSpec as P


BLK = "blk"
DIR = "dir"
VMEM = pltpu.VMEM
SMEM = pltpu.SMEM

COURANT = 0.15
WIND_GROWTH = 0.15
DAMP_RATE = 0.5
STEEP_COEF = 0.01
STOKES_SCALE = 0.15
RATIO_STEP = 1.1

LANES = 128
BANDS = 4
MIB = 1 << 20
FACES = 36
PITCH = 24
ROWS = 16
CUR_X, CUR_Y, WIND_X, WIND_Y, ICE = 0, 24, 48, 64, 80


def vmem_specs(count):
    return [pl.BlockSpec(memory_space=VMEM)] * count


def lane_of(shape):
    return lax.broadcasted_iota(jnp.int32, shape, len(shape) - 1)


def outgoing_kernel(
    bins,
    freqs,
    at_ref,
    cur_hbm,
    wind_hbm,
    ice_hbm,
    spec_hbm,
    speed_hbm,
    slot_hbm,
    out_ref,
    pair_ref,
    next_ref,
    cur_ref,
    wind_ref,
    ice_ref,
    spec_ref,
    speed_ref,
    slot_ref,
    x_ref,
    sems,
):
    sources = (cur_hbm, wind_hbm, ice_hbm, slot_hbm, speed_hbm, spec_hbm)
    targets = (cur_ref, wind_ref, ice_ref, slot_ref, speed_ref, spec_ref)
    copies = [pltpu.make_async_copy(a, b, sems.at[i]) for i, (a, b) in enumerate(zip(sources, targets))]
    for copy in copies:
        copy.start()
    for copy in copies[:3]:
        copy.wait()
    for c in range(2):
        for r in range(ROWS):
            x_ref[c, r : r + 1, :] = wind_ref[c : c + 1, LANES * r : LANES * (r + 1)]
    lane = lane_of((ROWS, LANES))

    def put(s, values, start):
        return pltpu.roll(values, (start - ROWS * s) % LANES, 1)

    for s in range(8):
        row = jnp.where(lane < CUR_Y, put(s, cur_ref[0], CUR_X + 1), put(s, cur_ref[1], CUR_Y))
        row = jnp.where(lane < WIND_X, row, put(s, x_ref[0], WIND_X))
        row = jnp.where(lane < WIND_Y, row, put(s, x_ref[1], WIND_Y))
        row = jnp.where(lane < ICE, row, put(s, ice_ref[...], ICE))
        out_ref[pl.ds(s, ROWS, stride=8), :] = row
    whole = out_ref[...]
    wide = lane_of((LANES, LANES))
    before = pltpu.roll(pltpu.roll(whole, 1, 0), LANES - ROWS, 1)
    after = pltpu.roll(pltpu.roll(whole, LANES - 1, 0), ROWS, 1)
    whole = jnp.where(wide == CUR_X, before, whole)
    out_ref[...] = jnp.where(wide == CUR_X + ROWS + 1, after, whole)
    odd = at_ref[0] >= BANDS
    for copy in copies[3:]:
        copy.wait()

    def trade(start, stop, first, last):
        pair_ref[start:stop, :] = jnp.where(odd, first, last)
        next_ref[start:stop, :] = jnp.where(odd, last, first)

    for source, start, count in ((spec_ref, 0, bins), (speed_ref, bins, freqs)):
        trade(start, start + count, source[pl.ds(0, count, stride=ROWS), :], source[pl.ds(ROWS - 1, count, stride=ROWS), :])
    sea = jnp.where(slot_ref[...] >= 0, 1.0, 0.0)
    sea = [jnp.broadcast_to(sea[r : r + 1, :], (8, LANES)) for r in (0, ROWS - 1)]
    trade(bins + freqs, bins + freqs + 8, *sea)


def move_kernel(
    dirs,
    freqs,
    at_ref,
    trig_ref,
    got_ref,
    spec_ref,
    speed_ref,
    slot_ref,
    stored_ref,
    parts_ref,
    cell_ref,
    turned_ref,
    sx_ref,
    sy_ref,
    sw_ref,
    moved_ref,
    flux_ref,
    sems,
):
    shape = (ROWS, LANES)
    row, lane = lax.broadcasted_iota(jnp.int32, shape, 0), lane_of(shape)
    turned_ref[...] = got_ref[...].T

    def shifted_down(values):
        return pltpu.roll(values, 1, 0)

    def next_y(values):
        return pltpu.roll(values, LANES - 1, 1)

    slots = slot_ref[...]
    sea = jnp.where(slots >= 0, 1.0, 0.0)
    half = 0.5 * COURANT
    open_x = jnp.where(row > 0, half * sea * shifted_down(sea), 0.0)
    open_y = jnp.where(lane < LANES - 1, half * sea * next_y(sea), 0.0)
    flow_x = open_x * (turned_ref[CUR_X : CUR_X + ROWS, :] + turned_ref[CUR_X + 1 : CUR_X + ROWS + 1, :])
    cur_y = turned_ref[CUR_Y : CUR_Y + ROWS, :]
    flow_y = open_y * (cur_y + next_y(cur_y))
    flow_w = pltpu.roll(flow_y, 1, 1)
    open_w = pltpu.roll(open_y, 1, 1)

    owner, place = jnp.maximum(slots, 0) // 16, jnp.where(slots >= 0, slots % 16, -1)
    wind_x, wind_y, ice = (jnp.zeros(shape, jnp.float32) for _ in range(3))
    for s in range(16):
        here = place == s

        def picked(start, old):
            table = jnp.broadcast_to(turned_ref[start + s : start + s + 1, :], shape)
            return jnp.where(here, jnp.take_along_axis(table, owner, axis=1), old)

        wind_x, wind_y, ice = picked(WIND_X, wind_x), picked(WIND_Y, wind_y), picked(ICE, ice)
    gain = WIND_GROWTH * (1.0 - ice)
    cell_ref[0:16, :] = wind_x
    cell_ref[16:32, :] = wind_y
    cell_ref[32:48, :] = gain
    cell_ref[56:72, :] = sea
    for side, x in enumerate((CUR_X, CUR_X + ROWS)):
        cell_ref[48 + side : 49 + side, :] = turned_ref[x : x + 1, :] + turned_ref[x + 1 : x + 2, :]

    def faces(k, _):
        base = pl.multiple_of(k * ROWS, ROWS)
        speed = speed_ref[pl.ds(base, ROWS), :]
        sx_ref[pl.ds(base, ROWS), :] = open_x * (speed + shifted_down(speed))
        sy_ref[pl.ds(base, ROWS), :] = open_y * (speed + next_y(speed))
        sw_ref[pl.ds(base, ROWS), :] = open_w * (speed + pltpu.roll(speed, 1, 1))
        return 0

    lax.fori_loop(0, freqs, faces, 0, unroll=FACES)

    zero = jnp.zeros(shape, jnp.float32)
    for k in range(freqs):
        flux_ref[k * PITCH + ROWS : (k + 1) * PITCH, :] = jnp.zeros((PITCH - ROWS, LANES), jnp.float32)
    at = at_ref[0] % BANDS

    def out_copy(j):
        part = pl.ds(pl.multiple_of(j * (freqs * ROWS), ROWS), freqs * ROWS)
        return pltpu.make_async_copy(moved_ref.at[part, :], stored_ref.at[part, :], sems.at[j])

    def direction(j, sums):
        moment, stress_x, stress_y, drift_x, drift_y, damp_x, damp_y = sums
        cosine, sine = trig_ref[at, j], trig_ref[at, dirs + j]
        start = pl.multiple_of(j * (freqs * ROWS), ROWS)
        second, third, fourth = zero, zero, zero
        for k in range(freqs):
            face = slice(k * ROWS, (k + 1) * ROWS)
            energy = spec_ref[pl.ds(start + k * ROWS, ROWS), :]
            lower = shifted_down(energy) if k == 0 else spec_ref[pl.ds(start + (k * ROWS - 1), ROWS), :]
            u = sx_ref[face, :] * cosine + flow_x
            below = u * jnp.where(u > 0.0, lower, energy)
            flux_ref[k * PITCH : k * PITCH + ROWS, :] = below
            above = flux_ref[k * PITCH + 1 : k * PITCH + ROWS + 1, :]
            v = sy_ref[face, :] * sine + flow_y
            right = v * jnp.where(v > 0.0, energy, next_y(energy))
            w = sw_ref[face, :] * sine + flow_w
            left = w * jnp.where(w > 0.0, pltpu.roll(energy, 1, 1), energy)
            moved = energy - ((above - below) + (right - left))
            moved_ref[pl.ds(start + k * ROWS, ROWS), :] = moved
            second = second * (RATIO_STEP**-2) + moved
            third = third * (RATIO_STEP**-3) + moved
            fourth = fourth * (RATIO_STEP**-4) + moved
        out_copy(j).start()
        second, third, fourth = sea * second, sea * third, sea * fourth
        wind_gain = gain * jnp.maximum(wind_x * cosine + wind_y * sine, 0.0)
        push = wind_gain * second
        drift = third + wind_gain * fourth
        return (
            moment + second,
            stress_x + cosine * push,
            stress_y + sine * push,
            drift_x + cosine * drift,
            drift_y + sine * drift,
            damp_x + cosine * fourth,
            damp_y + sine * fourth,
        )

    moment, stress_x, stress_y, drift_x, drift_y, damp_x, damp_y = lax.fori_loop(0, dirs, direction, (zero,) * 7)
    for c, (main, damped) in enumerate(((stress_x, zero), (stress_y, zero), (drift_x, damp_x), (drift_y, damp_y))):
        parts_ref[c, 0:16, :] = moment
        parts_ref[c, 16:32, :] = main
        parts_ref[c, 32:48, :] = damped
    for j in range(dirs):
        out_copy(j).wait()


def fix_kernel(
    dirs,
    freqs,
    at_ref,
    trig_ref,
    cell_ref,
    from_pair_ref,
    from_next_ref,
    to_pair_ref,
    to_next_ref,
    parts_ref,
    out_ref,
    fix_ref,
    behind_ref,
    ahead_ref,
):
    bins = dirs * freqs
    odd, at = at_ref[0] >= BANDS, at_ref[0] % BANDS
    power = lax.broadcasted_iota(jnp.int32, (freqs, LANES), 0).astype(jnp.float32) - (freqs - 1)
    weights = [jnp.exp(power * (p * math.log(RATIO_STEP))) for p in (2, 3, 4)]
    out_ref[...] = parts_ref[...]
    faces = (
        (0, 1.0, from_pair_ref, from_next_ref, to_pair_ref, to_next_ref),
        (ROWS - 1, -1.0, to_next_ref, to_pair_ref, from_next_ref, from_pair_ref),
    )
    for side, (row, sign, behind_odd, behind_even, ahead_odd, ahead_even) in enumerate(faces):
        behind_ref[...] = jnp.where(odd, behind_odd[...], behind_even[...])
        ahead_ref[...] = jnp.where(odd, ahead_odd[...], ahead_even[...])
        mask = slice(bins + freqs, bins + freqs + 1)
        opened = (sign * 0.5 * COURANT) * behind_ref[mask, :] * ahead_ref[mask, :]
        flow = opened * cell_ref[48 + side : 49 + side, :]
        speed = opened * (behind_ref[bins : bins + freqs, :] + ahead_ref[bins : bins + freqs, :])
        wind_x, wind_y, gain = (cell_ref[r : r + 1, :] for r in (row, 16 + row, 32 + row))
        moment, stress_x, stress_y, drift_x, drift_y, damp_x, damp_y = (jnp.zeros((1, LANES), jnp.float32),) * 7
        for j in range(dirs):
            cosine, sine = trig_ref[at, j], trig_ref[at, dirs + j]
            u = speed * cosine + flow
            part = slice(j * freqs, (j + 1) * freqs)
            flux = u * jnp.where(sign * u > 0.0, behind_ref[part, :], ahead_ref[part, :])
            fix_ref[side, part, :] = flux
            second, third, fourth = (jnp.sum(w * flux, axis=0, keepdims=True) for w in weights)
            wind_gain = gain * jnp.maximum(wind_x * cosine + wind_y * sine, 0.0)
            push = wind_gain * second
            drift = third + wind_gain * fourth
            moment += second
            stress_x += cosine * push
            stress_y += sine * push
            drift_x += cosine * drift
            drift_y += sine * drift
            damp_x += cosine * fourth
            damp_y += sine * fourth
        for c, (main, damped) in enumerate(((stress_x, None), (stress_y, None), (drift_x, damp_x), (drift_y, damp_y))):
            out_ref[c, row : row + 1, :] += moment
            out_ref[c, 16 + row : 17 + row, :] += main
            if damped is not None:
                out_ref[c, 32 + row : 33 + row, :] += damped


def forcing_kernel(at_ref, parts_ref, damping_ref, out_ref):
    parts = (parts_ref[0] + parts_ref[1]) + (parts_ref[2] + parts_ref[3])
    steepness = STEEP_COEF * parts[0:16]
    damping = DAMP_RATE * steepness / (1.0 + steepness)
    damping_ref[...] = damping
    own = parts[16:32] - damping * parts[32:48]
    own = jnp.where(at_ref[0] % BANDS < 2, 1.0, STOKES_SCALE) * own
    out_ref[...] = jnp.concatenate([own, jnp.zeros((LANES - ROWS, LANES), jnp.float32)], axis=0).T


def update_kernel(dirs, freqs, at_ref, trig_ref, moved_ref, cell_ref, damping_ref, fix_ref, out_ref):
    j, at = pl.program_id(0), at_ref[0] % BANDS
    cosine, sine = trig_ref[at, j], trig_ref[at, dirs + j]
    wind = jnp.maximum(cell_ref[0:16, :] * cosine + cell_ref[16:32, :] * sine, 0.0)
    sea = cell_ref[56:72, :]
    growth = sea * (cell_ref[32:48, :] * wind - damping_ref[...])
    row = lax.broadcasted_iota(jnp.int32, (ROWS, LANES), 0)
    for k in range(freqs):
        ratio = RATIO_STEP ** (k - freqs + 1)
        first, last = (jnp.broadcast_to(fix_ref[side, pl.ds(j * freqs + k, 1), :], (ROWS, LANES)) for side in (0, 1))
        edge = jnp.where(row == 0, first, jnp.where(row == ROWS - 1, last, 0.0))
        moved = moved_ref[k * ROWS : (k + 1) * ROWS, :] + edge
        out_ref[k * ROWS : (k + 1) * ROWS, :] = moved * (sea + ratio * growth)


def row_kernel(got_ref, out_ref):
    lane = lane_of((ROWS, LANES))
    row = got_ref[pl.ds(0, ROWS, stride=8), :]
    for s in range(1, 8):
        row = jnp.where(lane < ROWS * s, row, pltpu.roll(got_ref[pl.ds(s, ROWS, stride=8), :], ROWS * s, 1))
    out_ref[...] = row


def f32(*shape):
    return jax.ShapeDtypeStruct(shape, jnp.float32)


def near(*shape):
    return VMEM(shape, jnp.float32)


def held(value):
    return pltpu.with_memory_space_constraint(value, VMEM)


def one_step(spectrum, group_speed, ocean_current, route_slot, wind_vector, ice_cover):
    dirs, freqs, _, _ = spectrum.shape
    bands, blocks = lax.axis_size(DIR), lax.axis_size(BLK)
    bins = dirs * freqs
    at = (lax.axis_index(DIR) + bands * (lax.axis_index(BLK) & 1)).astype(jnp.int32).reshape(1)
    angles = (2.0 * np.pi * np.arange(bands * dirs, dtype=np.float32) / np.float32(bands * dirs)).astype(np.float32)
    angles = angles.astype(np.float64).reshape(bands, dirs)
    trig = jnp.asarray(np.concatenate([np.cos(angles), np.sin(angles)], axis=1).astype(np.float32))
    smem = pl.BlockSpec(memory_space=SMEM)

    def far(value):
        return pltpu.with_memory_space_constraint(value, pltpu.HBM)

    flat, speed = spectrum.reshape(bins * ROWS, LANES), group_speed.reshape(freqs * ROWS, LANES)
    edge = near(bins + freqs + 8, LANES)
    messages, to_pair, to_next = pl.pallas_call(
        lambda *refs: outgoing_kernel(bins, freqs, *refs),
        out_shape=(near(LANES, LANES), edge, edge),
        in_specs=[smem] + [pl.BlockSpec(memory_space=pltpu.HBM)] * 6,
        out_specs=tuple(vmem_specs(3)),
        scratch_shapes=[
            VMEM((2, ROWS, LANES), jnp.float32),
            VMEM((2, ROWS * LANES), jnp.float32),
            VMEM((ROWS, LANES), jnp.float32),
            VMEM((bins * ROWS, LANES), jnp.float32),
            VMEM((freqs * ROWS, LANES), jnp.float32),
            VMEM((ROWS, LANES), jnp.int32),
            VMEM((2, ROWS, LANES), jnp.float32),
            pltpu.SemaphoreType.DMA((6,)),
        ],
        name="outgoing",
        compiler_params=pltpu.CompilerParams(vmem_limit_bytes=8 * MIB),
    )(
        at,
        far(ocean_current.reshape(2, ROWS, LANES)),
        far(wind_vector.reshape(2, ROWS * LANES)),
        far(ice_cover.reshape(ROWS, LANES)),
        far(flat),
        far(speed),
        far(route_slot),
    )
    flat, speed = held(flat), held(speed)
    pairs = [(i, i + 1) for i in range(0, blocks, 2)]
    nexts = [(i, i + 1) for i in range(1, blocks - 1, 2)]
    got = held(lax.all_to_all(messages, BLK, 0, 0, tiled=True))
    from_next = held(lax.ppermute(to_next, BLK, nexts + [(j, i) for i, j in nexts]))
    from_pair = held(lax.ppermute(to_pair, BLK, pairs + [(j, i) for i, j in pairs]))
    move = pl.pallas_call(
        lambda *refs: move_kernel(dirs, freqs, *refs),
        out_shape=(pltpu.HBM((bins * ROWS, LANES), jnp.float32), near(bands, 48, LANES), near(72, LANES)),
        in_specs=[smem, smem] + vmem_specs(4),
        out_specs=(pl.BlockSpec(memory_space=pltpu.HBM), *vmem_specs(2)),
        scratch_shapes=[
            VMEM((LANES, LANES), jnp.float32),
            VMEM((freqs * ROWS, LANES), jnp.float32),
            VMEM((freqs * ROWS, LANES), jnp.float32),
            VMEM((freqs * ROWS, LANES), jnp.float32),
            VMEM((bins * ROWS, LANES), jnp.float32),
            VMEM((freqs * PITCH, LANES), jnp.float32),
            pltpu.SemaphoreType.DMA((dirs,)),
        ],
        name="move",
        compiler_params=pltpu.CompilerParams(vmem_limit_bytes=8 * MIB),
    )
    moved, parts, cell = move(at, trig, got, flat, speed, route_slot)
    parts, fixes = pl.pallas_call(
        lambda *refs: fix_kernel(dirs, freqs, *refs),
        out_shape=(near(bands, 48, LANES), near(2, bins, LANES)),
        in_specs=[smem, smem] + vmem_specs(6),
        out_specs=tuple(vmem_specs(2)),
        scratch_shapes=[VMEM((bins + freqs + 8, LANES), jnp.float32), VMEM((bins + freqs + 8, LANES), jnp.float32)],
        name="fix",
        compiler_params=pltpu.CompilerParams(vmem_limit_bytes=4 * MIB),
    )(at, trig, cell, from_pair, from_next, to_pair, to_next, parts)

    parts = held(lax.all_to_all(parts, DIR, 0, 0, tiled=True))
    damping, own = pl.pallas_call(
        forcing_kernel,
        out_shape=(near(ROWS, LANES), near(LANES, LANES)),
        in_specs=[smem] + vmem_specs(1),
        out_specs=tuple(vmem_specs(2)),
        name="forcing",
        compiler_params=pltpu.CompilerParams(vmem_limit_bytes=4 * MIB),
    )(at, parts)
    ocean = held(lax.all_to_all(own, BLK, 0, 0, tiled=True))
    result = pl.pallas_call(
        lambda *refs: update_kernel(dirs, freqs, *refs),
        out_shape=f32(bins * ROWS, LANES),
        grid=(dirs,),
        in_specs=[smem, smem, pl.BlockSpec((freqs * ROWS, LANES), lambda j: (j, 0))] + vmem_specs(3),
        out_specs=pl.BlockSpec((freqs * ROWS, LANES), lambda j: (j, 0)),
        name="update",
        compiler_params=pltpu.CompilerParams(vmem_limit_bytes=4 * MIB),
        cost_estimate=pl.CostEstimate(flops=3 * bins * ROWS * LANES, bytes_accessed=8 * bins * ROWS * LANES, transcendentals=0),
    )(at, trig, pltpu.with_memory_space_constraint(moved, pltpu.HBM), cell, damping, fixes)
    ocean = pl.pallas_call(
        row_kernel,
        out_shape=f32(ROWS, LANES),
        in_specs=vmem_specs(1),
        out_specs=vmem_specs(1)[0],
        name="rows",
        compiler_params=pltpu.CompilerParams(vmem_limit_bytes=4 * MIB),
    )(ocean)
    return (result.reshape(spectrum.shape), ocean.reshape(1, 1, ROWS * LANES))


def solution(mesh):
    return jax.shard_map(
        one_step,
        mesh=mesh,
        in_specs=(
            P(DIR, None, BLK, None),
            P(None, BLK, None),
            P(None, BLK, None),
            P(BLK, None),
            P(BLK, None, None),
            P(BLK, None),
        ),
        out_specs=(P(DIR, None, BLK, None), P(DIR, BLK, None)),
        check_vma=False,
    )
```

```python
import math

import jax
import jax.numpy as jnp
import numpy as np
from jax import lax
from jax.experimental import pallas as pl
from jax.experimental.pallas import tpu as pltpu
from jax.sharding import PartitionSpec as P


BLK = "blk"
DIR = "dir"
VMEM = pltpu.VMEM
SMEM = pltpu.SMEM

COURANT = 0.15
WIND_GROWTH = 0.15
DAMP_RATE = 0.5
STEEP_COEF = 0.01
STOKES_SCALE = 0.15
RATIO_STEP = 1.1

LANES = 128
BANDS = 4
MIB = 1 << 20
FACES = 36
PITCH = 24
ROWS = 16
CUR_X, CUR_Y, WIND_X, WIND_Y, ICE = 0, 24, 48, 64, 80


def vmem_specs(count):
    return [pl.BlockSpec(memory_space=VMEM)] * count


def lane_of(shape):
    return lax.broadcasted_iota(jnp.int32, shape, len(shape) - 1)


def outgoing_kernel(
    bins,
    freqs,
    at_ref,
    cur_hbm,
    wind_hbm,
    ice_hbm,
    spec_hbm,
    speed_hbm,
    slot_hbm,
    sent_hbm,
    pair_ref,
    next_ref,
    spec_ref,
    speed_ref,
    cur_ref,
    wind_ref,
    ice_ref,
    slot_ref,
    x_ref,
    out_ref,
    sems,
):
    sources = (cur_hbm, wind_hbm, ice_hbm, slot_hbm, speed_hbm, spec_hbm)
    targets = (cur_ref, wind_ref, ice_ref, slot_ref, speed_ref, spec_ref)
    copies = [pltpu.make_async_copy(a, b, sems.at[i]) for i, (a, b) in enumerate(zip(sources, targets))]
    for copy in copies:
        copy.start()
    for copy in copies[:3]:
        copy.wait()
    for c in range(2):
        for r in range(ROWS):
            x_ref[c, r : r + 1, :] = wind_ref[c : c + 1, LANES * r : LANES * (r + 1)]
    lane = lane_of((ROWS, LANES))

    def put(s, values, start):
        return pltpu.roll(values, (start - ROWS * s) % LANES, 1)

    for s in range(8):
        row = jnp.where(lane < CUR_Y, put(s, cur_ref[0], CUR_X + 1), put(s, cur_ref[1], CUR_Y))
        row = jnp.where(lane < WIND_X, row, put(s, x_ref[0], WIND_X))
        row = jnp.where(lane < WIND_Y, row, put(s, x_ref[1], WIND_Y))
        row = jnp.where(lane < ICE, row, put(s, ice_ref[...], ICE))
        out_ref[pl.ds(s, ROWS, stride=8), :] = row
    whole = out_ref[...]
    wide = lane_of((LANES, LANES))
    before = pltpu.roll(pltpu.roll(whole, 1, 0), LANES - ROWS, 1)
    after = pltpu.roll(pltpu.roll(whole, LANES - 1, 0), ROWS, 1)
    whole = jnp.where(wide == CUR_X, before, whole)
    out_ref[...] = jnp.where(wide == CUR_X + ROWS + 1, after, whole)
    sending = pltpu.make_async_copy(out_ref, sent_hbm, sems.at[len(sources)])
    sending.start()
    odd = at_ref[0] >= BANDS
    for copy in copies[3:]:
        copy.wait()

    def trade(start, stop, first, last):
        pair_ref[start:stop, :] = jnp.where(odd, first, last)
        next_ref[start:stop, :] = jnp.where(odd, last, first)

    for source, start, count in ((spec_ref, 0, bins), (speed_ref, bins, freqs)):
        trade(start, start + count, source[pl.ds(0, count, stride=ROWS), :], source[pl.ds(ROWS - 1, count, stride=ROWS), :])
    sea = jnp.where(slot_ref[...] >= 0, 1.0, 0.0)
    sea = [jnp.broadcast_to(sea[r : r + 1, :], (8, LANES)) for r in (0, ROWS - 1)]
    trade(bins + freqs, bins + freqs + 8, *sea)
    sending.wait()


def move_kernel(
    dirs,
    freqs,
    at_ref,
    trig_ref,
    got_ref,
    spec_ref,
    speed_ref,
    slot_ref,
    stored_ref,
    parts_ref,
    cell_ref,
    turned_ref,
    sx_ref,
    sy_ref,
    sw_ref,
    moved_ref,
    flux_ref,
    sems,
):
    shape = (ROWS, LANES)
    row, lane = lax.broadcasted_iota(jnp.int32, shape, 0), lane_of(shape)
    turned_ref[...] = got_ref[...].T

    def shifted_down(values):
        return pltpu.roll(values, 1, 0)

    def next_y(values):
        return pltpu.roll(values, LANES - 1, 1)

    slots = slot_ref[...]
    sea = jnp.where(slots >= 0, 1.0, 0.0)
    half = 0.5 * COURANT
    open_x = jnp.where(row > 0, half * sea * shifted_down(sea), 0.0)
    open_y = jnp.where(lane < LANES - 1, half * sea * next_y(sea), 0.0)
    flow_x = open_x * (turned_ref[CUR_X : CUR_X + ROWS, :] + turned_ref[CUR_X + 1 : CUR_X + ROWS + 1, :])
    cur_y = turned_ref[CUR_Y : CUR_Y + ROWS, :]
    flow_y = open_y * (cur_y + next_y(cur_y))
    flow_w = pltpu.roll(flow_y, 1, 1)
    open_w = pltpu.roll(open_y, 1, 1)

    owner, place = jnp.maximum(slots, 0) // 16, jnp.where(slots >= 0, slots % 16, -1)
    wind_x, wind_y, ice = (jnp.zeros(shape, jnp.float32) for _ in range(3))
    for s in range(16):
        here = place == s

        def picked(start, old):
            table = jnp.broadcast_to(turned_ref[start + s : start + s + 1, :], shape)
            return jnp.where(here, jnp.take_along_axis(table, owner, axis=1), old)

        wind_x, wind_y, ice = picked(WIND_X, wind_x), picked(WIND_Y, wind_y), picked(ICE, ice)
    gain = WIND_GROWTH * (1.0 - ice)
    cell_ref[0:16, :] = wind_x
    cell_ref[16:32, :] = wind_y
    cell_ref[32:48, :] = gain
    cell_ref[56:72, :] = sea
    for side, x in enumerate((CUR_X, CUR_X + ROWS)):
        cell_ref[48 + side : 49 + side, :] = turned_ref[x : x + 1, :] + turned_ref[x + 1 : x + 2, :]

    def faces(k, _):
        base = pl.multiple_of(k * ROWS, ROWS)
        speed = speed_ref[pl.ds(base, ROWS), :]
        sx_ref[pl.ds(base, ROWS), :] = open_x * (speed + shifted_down(speed))
        sy_ref[pl.ds(base, ROWS), :] = open_y * (speed + next_y(speed))
        sw_ref[pl.ds(base, ROWS), :] = open_w * (speed + pltpu.roll(speed, 1, 1))
        return 0

    lax.fori_loop(0, freqs, faces, 0, unroll=FACES)

    zero = jnp.zeros(shape, jnp.float32)
    for k in range(freqs):
        flux_ref[k * PITCH + ROWS : (k + 1) * PITCH, :] = jnp.zeros((PITCH - ROWS, LANES), jnp.float32)
    at = at_ref[0] % BANDS

    def out_copy(j):
        part = pl.ds(pl.multiple_of(j * (freqs * ROWS), ROWS), freqs * ROWS)
        return pltpu.make_async_copy(moved_ref.at[part, :], stored_ref.at[part, :], sems.at[j])

    def direction(j, sums):
        moment, stress_x, stress_y, drift_x, drift_y, damp_x, damp_y = sums
        cosine, sine = trig_ref[at, j], trig_ref[at, dirs + j]
        start = pl.multiple_of(j * (freqs * ROWS), ROWS)
        second, third, fourth = zero, zero, zero
        for k in range(freqs):
            face = slice(k * ROWS, (k + 1) * ROWS)
            energy = spec_ref[pl.ds(start + k * ROWS, ROWS), :]
            lower = shifted_down(energy) if k == 0 else spec_ref[pl.ds(start + (k * ROWS - 1), ROWS), :]
            u = sx_ref[face, :] * cosine + flow_x
            below = u * jnp.where(u > 0.0, lower, energy)
            flux_ref[k * PITCH : k * PITCH + ROWS, :] = below
            above = flux_ref[k * PITCH + 1 : k * PITCH + ROWS + 1, :]
            v = sy_ref[face, :] * sine + flow_y
            right = v * jnp.where(v > 0.0, energy, next_y(energy))
            w = sw_ref[face, :] * sine + flow_w
            left = w * jnp.where(w > 0.0, pltpu.roll(energy, 1, 1), energy)
            moved = energy - ((above - below) + (right - left))
            moved_ref[pl.ds(start + k * ROWS, ROWS), :] = moved
            second = second * (RATIO_STEP**-2) + moved
            third = third * (RATIO_STEP**-3) + moved
            fourth = fourth * (RATIO_STEP**-4) + moved
        out_copy(j).start()
        second, third, fourth = sea * second, sea * third, sea * fourth
        wind_gain = gain * jnp.maximum(wind_x * cosine + wind_y * sine, 0.0)
        push = wind_gain * second
        drift = third + wind_gain * fourth
        return (
            moment + second,
            stress_x + cosine * push,
            stress_y + sine * push,
            drift_x + cosine * drift,
            drift_y + sine * drift,
            damp_x + cosine * fourth,
            damp_y + sine * fourth,
        )

    moment, stress_x, stress_y, drift_x, drift_y, damp_x, damp_y = lax.fori_loop(0, dirs, direction, (zero,) * 7)
    for c, (main, damped) in enumerate(((stress_x, zero), (stress_y, zero), (drift_x, damp_x), (drift_y, damp_y))):
        parts_ref[c, 0:16, :] = moment
        parts_ref[c, 16:32, :] = main
        parts_ref[c, 32:48, :] = damped
    for j in range(dirs):
        out_copy(j).wait()


def fix_kernel(
    dirs,
    freqs,
    at_ref,
    trig_ref,
    cell_ref,
    from_pair_ref,
    from_next_ref,
    to_pair_ref,
    to_next_ref,
    parts_ref,
    out_ref,
    fix_ref,
    behind_ref,
    ahead_ref,
):
    bins = dirs * freqs
    odd, at = at_ref[0] >= BANDS, at_ref[0] % BANDS
    power = lax.broadcasted_iota(jnp.int32, (freqs, LANES), 0).astype(jnp.float32) - (freqs - 1)
    weights = [jnp.exp(power * (p * math.log(RATIO_STEP))) for p in (2, 3, 4)]
    out_ref[...] = parts_ref[...]
    faces = (
        (0, 1.0, from_pair_ref, from_next_ref, to_pair_ref, to_next_ref),
        (ROWS - 1, -1.0, to_next_ref, to_pair_ref, from_next_ref, from_pair_ref),
    )
    for side, (row, sign, behind_odd, behind_even, ahead_odd, ahead_even) in enumerate(faces):
        behind_ref[...] = jnp.where(odd, behind_odd[...], behind_even[...])
        ahead_ref[...] = jnp.where(odd, ahead_odd[...], ahead_even[...])
        mask = slice(bins + freqs, bins + freqs + 1)
        opened = (sign * 0.5 * COURANT) * behind_ref[mask, :] * ahead_ref[mask, :]
        flow = opened * cell_ref[48 + side : 49 + side, :]
        speed = opened * (behind_ref[bins : bins + freqs, :] + ahead_ref[bins : bins + freqs, :])
        wind_x, wind_y, gain = (cell_ref[r : r + 1, :] for r in (row, 16 + row, 32 + row))
        moment, stress_x, stress_y, drift_x, drift_y, damp_x, damp_y = (jnp.zeros((1, LANES), jnp.float32),) * 7
        for j in range(dirs):
            cosine, sine = trig_ref[at, j], trig_ref[at, dirs + j]
            u = speed * cosine + flow
            part = slice(j * freqs, (j + 1) * freqs)
            flux = u * jnp.where(sign * u > 0.0, behind_ref[part, :], ahead_ref[part, :])
            fix_ref[side, part, :] = flux
            second, third, fourth = (jnp.sum(w * flux, axis=0, keepdims=True) for w in weights)
            wind_gain = gain * jnp.maximum(wind_x * cosine + wind_y * sine, 0.0)
            push = wind_gain * second
            drift = third + wind_gain * fourth
            moment += second
            stress_x += cosine * push
            stress_y += sine * push
            drift_x += cosine * drift
            drift_y += sine * drift
            damp_x += cosine * fourth
            damp_y += sine * fourth
        for c, (main, damped) in enumerate(((stress_x, None), (stress_y, None), (drift_x, damp_x), (drift_y, damp_y))):
            out_ref[c, row : row + 1, :] += moment
            out_ref[c, 16 + row : 17 + row, :] += main
            if damped is not None:
                out_ref[c, 32 + row : 33 + row, :] += damped


def forcing_kernel(at_ref, parts_ref, damping_ref, out_ref):
    parts = (parts_ref[0] + parts_ref[1]) + (parts_ref[2] + parts_ref[3])
    steepness = STEEP_COEF * parts[0:16]
    damping = DAMP_RATE * steepness / (1.0 + steepness)
    damping_ref[...] = damping
    own = parts[16:32] - damping * parts[32:48]
    own = jnp.where(at_ref[0] % BANDS < 2, 1.0, STOKES_SCALE) * own
    out_ref[...] = jnp.concatenate([own, jnp.zeros((LANES - ROWS, LANES), jnp.float32)], axis=0).T


def update_kernel(dirs, freqs, at_ref, trig_ref, moved_ref, cell_ref, damping_ref, fix_ref, out_ref):
    j, at = pl.program_id(0), at_ref[0] % BANDS
    cosine, sine = trig_ref[at, j], trig_ref[at, dirs + j]
    wind = jnp.maximum(cell_ref[0:16, :] * cosine + cell_ref[16:32, :] * sine, 0.0)
    sea = cell_ref[56:72, :]
    growth = sea * (cell_ref[32:48, :] * wind - damping_ref[...])
    row = lax.broadcasted_iota(jnp.int32, (ROWS, LANES), 0)
    for k in range(freqs):
        ratio = RATIO_STEP ** (k - freqs + 1)
        first, last = (jnp.broadcast_to(fix_ref[side, pl.ds(j * freqs + k, 1), :], (ROWS, LANES)) for side in (0, 1))
        edge = jnp.where(row == 0, first, jnp.where(row == ROWS - 1, last, 0.0))
        moved = moved_ref[k * ROWS : (k + 1) * ROWS, :] + edge
        out_ref[k * ROWS : (k + 1) * ROWS, :] = moved * (sea + ratio * growth)


def row_kernel(got_ref, out_ref):
    lane = lane_of((ROWS, LANES))
    row = got_ref[pl.ds(0, ROWS, stride=8), :]
    for s in range(1, 8):
        row = jnp.where(lane < ROWS * s, row, pltpu.roll(got_ref[pl.ds(s, ROWS, stride=8), :], ROWS * s, 1))
    out_ref[...] = row


def f32(*shape):
    return jax.ShapeDtypeStruct(shape, jnp.float32)


def near(*shape):
    return VMEM(shape, jnp.float32)


def held(value):
    return pltpu.with_memory_space_constraint(value, VMEM)


def one_step(spectrum, group_speed, ocean_current, route_slot, wind_vector, ice_cover):
    dirs, freqs, _, _ = spectrum.shape
    bands, blocks = lax.axis_size(DIR), lax.axis_size(BLK)
    bins = dirs * freqs
    at = (lax.axis_index(DIR) + bands * (lax.axis_index(BLK) & 1)).astype(jnp.int32).reshape(1)
    angles = (2.0 * np.pi * np.arange(bands * dirs, dtype=np.float32) / np.float32(bands * dirs)).astype(np.float32)
    angles = angles.astype(np.float64).reshape(bands, dirs)
    trig = jnp.asarray(np.concatenate([np.cos(angles), np.sin(angles)], axis=1).astype(np.float32))
    smem = pl.BlockSpec(memory_space=SMEM)

    def far(value):
        return pltpu.with_memory_space_constraint(value, pltpu.HBM)

    flat, speed = spectrum.reshape(bins * ROWS, LANES), group_speed.reshape(freqs * ROWS, LANES)
    edge = near(bins + freqs + 8, LANES)
    messages, to_pair, to_next, flat, speed = pl.pallas_call(
        lambda *refs: outgoing_kernel(bins, freqs, *refs),
        out_shape=(
            pltpu.HBM((LANES, LANES), jnp.float32),
            edge,
            edge,
            near(bins * ROWS, LANES),
            near(freqs * ROWS, LANES),
        ),
        in_specs=[smem] + [pl.BlockSpec(memory_space=pltpu.HBM)] * 6,
        out_specs=(pl.BlockSpec(memory_space=pltpu.HBM), *vmem_specs(4)),
        scratch_shapes=[
            VMEM((2, ROWS, LANES), jnp.float32),
            VMEM((2, ROWS * LANES), jnp.float32),
            VMEM((ROWS, LANES), jnp.float32),
            VMEM((ROWS, LANES), jnp.int32),
            VMEM((2, ROWS, LANES), jnp.float32),
            VMEM((LANES, LANES), jnp.float32),
            pltpu.SemaphoreType.DMA((7,)),
        ],
        name="outgoing",
        compiler_params=pltpu.CompilerParams(vmem_limit_bytes=8 * MIB),
    )(
        at,
        far(ocean_current.reshape(2, ROWS, LANES)),
        far(wind_vector.reshape(2, ROWS * LANES)),
        far(ice_cover.reshape(ROWS, LANES)),
        far(flat),
        far(speed),
        far(route_slot),
    )
    pairs = [(i, i + 1) for i in range(0, blocks, 2)]
    nexts = [(i, i + 1) for i in range(1, blocks - 1, 2)]
    got = held(lax.all_to_all(messages, BLK, 0, 0, tiled=True))
    from_next = held(lax.ppermute(to_next, BLK, nexts + [(j, i) for i, j in nexts]))
    from_pair = held(lax.ppermute(to_pair, BLK, pairs + [(j, i) for i, j in pairs]))
    move = pl.pallas_call(
        lambda *refs: move_kernel(dirs, freqs, *refs),
        out_shape=(pltpu.HBM((bins * ROWS, LANES), jnp.float32), near(bands, 48, LANES), near(72, LANES)),
        in_specs=[smem, smem] + vmem_specs(4),
        out_specs=(pl.BlockSpec(memory_space=pltpu.HBM), *vmem_specs(2)),
        scratch_shapes=[
            VMEM((LANES, LANES), jnp.float32),
            VMEM((freqs * ROWS, LANES), jnp.float32),
            VMEM((freqs * ROWS, LANES), jnp.float32),
            VMEM((freqs * ROWS, LANES), jnp.float32),
            VMEM((bins * ROWS, LANES), jnp.float32),
            VMEM((freqs * PITCH, LANES), jnp.float32),
            pltpu.SemaphoreType.DMA((dirs,)),
        ],
        name="move",
        compiler_params=pltpu.CompilerParams(vmem_limit_bytes=8 * MIB),
    )
    moved, parts, cell = move(at, trig, got, flat, speed, route_slot)
    parts, fixes = pl.pallas_call(
        lambda *refs: fix_kernel(dirs, freqs, *refs),
        out_shape=(near(bands, 48, LANES), near(2, bins, LANES)),
        in_specs=[smem, smem] + vmem_specs(6),
        out_specs=tuple(vmem_specs(2)),
        scratch_shapes=[VMEM((bins + freqs + 8, LANES), jnp.float32), VMEM((bins + freqs + 8, LANES), jnp.float32)],
        name="fix",
        compiler_params=pltpu.CompilerParams(vmem_limit_bytes=4 * MIB),
    )(at, trig, cell, from_pair, from_next, to_pair, to_next, parts)

    parts = held(lax.all_to_all(parts, DIR, 0, 0, tiled=True))
    damping, own = pl.pallas_call(
        forcing_kernel,
        out_shape=(near(ROWS, LANES), near(LANES, LANES)),
        in_specs=[smem] + vmem_specs(1),
        out_specs=tuple(vmem_specs(2)),
        name="forcing",
        compiler_params=pltpu.CompilerParams(vmem_limit_bytes=4 * MIB),
    )(at, parts)
    ocean = held(lax.all_to_all(own, BLK, 0, 0, tiled=True))
    result = pl.pallas_call(
        lambda *refs: update_kernel(dirs, freqs, *refs),
        out_shape=f32(bins * ROWS, LANES),
        grid=(dirs,),
        in_specs=[smem, smem, pl.BlockSpec((freqs * ROWS, LANES), lambda j: (j, 0))] + vmem_specs(3),
        out_specs=pl.BlockSpec((freqs * ROWS, LANES), lambda j: (j, 0)),
        name="update",
        compiler_params=pltpu.CompilerParams(vmem_limit_bytes=4 * MIB),
        cost_estimate=pl.CostEstimate(flops=3 * bins * ROWS * LANES, bytes_accessed=8 * bins * ROWS * LANES, transcendentals=0),
    )(at, trig, pltpu.with_memory_space_constraint(moved, pltpu.HBM), cell, damping, fixes)
    ocean = pl.pallas_call(
        row_kernel,
        out_shape=f32(ROWS, LANES),
        in_specs=vmem_specs(1),
        out_specs=vmem_specs(1)[0],
        name="rows",
        compiler_params=pltpu.CompilerParams(vmem_limit_bytes=4 * MIB),
    )(ocean)
    return (result.reshape(spectrum.shape), ocean.reshape(1, 1, ROWS * LANES))


def solution(mesh):
    return jax.shard_map(
        one_step,
        mesh=mesh,
        in_specs=(
            P(DIR, None, BLK, None),
            P(None, BLK, None),
            P(None, BLK, None),
            P(BLK, None),
            P(BLK, None, None),
            P(BLK, None),
        ),
        out_specs=(P(DIR, None, BLK, None), P(DIR, BLK, None)),
        check_vma=False,
    )
```

```python
import math

import jax
import jax.numpy as jnp
import numpy as np
from jax import lax
from jax.experimental import pallas as pl
from jax.experimental.pallas import tpu as pltpu
from jax.sharding import PartitionSpec as P


BLK = "blk"
DIR = "dir"
VMEM = pltpu.VMEM
SMEM = pltpu.SMEM

COURANT = 0.15
WIND_GROWTH = 0.15
DAMP_RATE = 0.5
STEEP_COEF = 0.01
STOKES_SCALE = 0.15
RATIO_STEP = 1.1

LANES = 128
BANDS = 4
MIB = 1 << 20
FACES = 36
PITCH = 24
ROWS = 16
CUR_X, CUR_Y, WIND_X, WIND_Y, ICE = 0, 24, 48, 64, 80


def vmem_specs(count):
    return [pl.BlockSpec(memory_space=VMEM)] * count


def lane_of(shape):
    return lax.broadcasted_iota(jnp.int32, shape, len(shape) - 1)


def outgoing_kernel(
    bins,
    freqs,
    at_ref,
    cur_hbm,
    wind_hbm,
    ice_hbm,
    spec_hbm,
    speed_hbm,
    slot_hbm,
    sent_hbm,
    pair_ref,
    next_ref,
    spec_ref,
    speed_ref,
    cur_ref,
    wind_ref,
    ice_ref,
    slot_ref,
    x_ref,
    out_ref,
    sems,
):
    sources = (cur_hbm, wind_hbm, ice_hbm, slot_hbm, speed_hbm, spec_hbm)
    targets = (cur_ref, wind_ref, ice_ref, slot_ref, speed_ref, spec_ref)
    copies = [pltpu.make_async_copy(a, b, sems.at[i]) for i, (a, b) in enumerate(zip(sources, targets))]
    for copy in copies:
        copy.start()
    for copy in copies[:3]:
        copy.wait()
    for c in range(2):
        for r in range(ROWS):
            x_ref[c, r : r + 1, :] = wind_ref[c : c + 1, LANES * r : LANES * (r + 1)]
    lane = lane_of((ROWS, LANES))

    def put(s, values, start):
        return pltpu.roll(values, (start - ROWS * s) % LANES, 1)

    for s in range(8):
        row = jnp.where(lane < CUR_Y, put(s, cur_ref[0], CUR_X + 1), put(s, cur_ref[1], CUR_Y))
        row = jnp.where(lane < WIND_X, row, put(s, x_ref[0], WIND_X))
        row = jnp.where(lane < WIND_Y, row, put(s, x_ref[1], WIND_Y))
        row = jnp.where(lane < ICE, row, put(s, ice_ref[...], ICE))
        out_ref[pl.ds(s, ROWS, stride=8), :] = row
    whole = out_ref[...]
    wide = lane_of((LANES, LANES))
    before = pltpu.roll(pltpu.roll(whole, 1, 0), LANES - ROWS, 1)
    after = pltpu.roll(pltpu.roll(whole, LANES - 1, 0), ROWS, 1)
    whole = jnp.where(wide == CUR_X, before, whole)
    out_ref[...] = jnp.where(wide == CUR_X + ROWS + 1, after, whole)
    sending = pltpu.make_async_copy(out_ref, sent_hbm, sems.at[len(sources)])
    sending.start()
    odd = at_ref[0] >= BANDS
    for copy in copies[3:]:
        copy.wait()

    def trade(start, stop, first, last):
        pair_ref[start:stop, :] = jnp.where(odd, first, last)
        next_ref[start:stop, :] = jnp.where(odd, last, first)

    for source, start, count in ((spec_ref, 0, bins), (speed_ref, bins, freqs)):
        trade(start, start + count, source[pl.ds(0, count, stride=ROWS), :], source[pl.ds(ROWS - 1, count, stride=ROWS), :])
    sea = jnp.where(slot_ref[...] >= 0, 1.0, 0.0)
    sea = [jnp.broadcast_to(sea[r : r + 1, :], (8, LANES)) for r in (0, ROWS - 1)]
    trade(bins + freqs, bins + freqs + 8, *sea)
    sending.wait()


def move_kernel(
    dirs,
    freqs,
    at_ref,
    trig_ref,
    got_ref,
    spec_ref,
    speed_ref,
    slot_ref,
    stored_ref,
    parts_ref,
    cell_ref,
    turned_ref,
    sx_ref,
    sy_ref,
    sw_ref,
    moved_ref,
    flux_ref,
    sems,
):
    shape = (ROWS, LANES)
    row, lane = lax.broadcasted_iota(jnp.int32, shape, 0), lane_of(shape)
    turned_ref[...] = got_ref[...].T

    def shifted_down(values):
        return pltpu.roll(values, 1, 0)

    def next_y(values):
        return pltpu.roll(values, LANES - 1, 1)

    slots = slot_ref[...]
    sea = jnp.where(slots >= 0, 1.0, 0.0)
    half = 0.5 * COURANT
    open_x = jnp.where(row > 0, half * sea * shifted_down(sea), 0.0)
    open_y = jnp.where(lane < LANES - 1, half * sea * next_y(sea), 0.0)
    flow_x = open_x * (turned_ref[CUR_X : CUR_X + ROWS, :] + turned_ref[CUR_X + 1 : CUR_X + ROWS + 1, :])
    cur_y = turned_ref[CUR_Y : CUR_Y + ROWS, :]
    flow_y = open_y * (cur_y + next_y(cur_y))
    flow_w = pltpu.roll(flow_y, 1, 1)
    open_w = pltpu.roll(open_y, 1, 1)

    owner, place = jnp.maximum(slots, 0) // 16, jnp.where(slots >= 0, slots % 16, -1)
    wind_x, wind_y, ice = (jnp.zeros(shape, jnp.float32) for _ in range(3))
    for s in range(16):
        here = place == s

        def picked(start, old):
            table = jnp.broadcast_to(turned_ref[start + s : start + s + 1, :], shape)
            return jnp.where(here, jnp.take_along_axis(table, owner, axis=1), old)

        wind_x, wind_y, ice = picked(WIND_X, wind_x), picked(WIND_Y, wind_y), picked(ICE, ice)
    gain = WIND_GROWTH * (1.0 - ice)
    cell_ref[0:16, :] = wind_x
    cell_ref[16:32, :] = wind_y
    cell_ref[32:48, :] = gain
    cell_ref[56:72, :] = sea
    for side, x in enumerate((CUR_X, CUR_X + ROWS)):
        cell_ref[48 + side : 49 + side, :] = turned_ref[x : x + 1, :] + turned_ref[x + 1 : x + 2, :]

    def faces(k, _):
        base = pl.multiple_of(k * ROWS, ROWS)
        speed = speed_ref[pl.ds(base, ROWS), :]
        sx_ref[pl.ds(base, ROWS), :] = open_x * (speed + shifted_down(speed))
        sy_ref[pl.ds(base, ROWS), :] = open_y * (speed + next_y(speed))
        sw_ref[pl.ds(base, ROWS), :] = open_w * (speed + pltpu.roll(speed, 1, 1))
        return 0

    lax.fori_loop(0, freqs, faces, 0, unroll=FACES)

    zero = jnp.zeros(shape, jnp.float32)
    for k in range(freqs):
        flux_ref[k * PITCH + ROWS : (k + 1) * PITCH, :] = jnp.zeros((PITCH - ROWS, LANES), jnp.float32)
    at = at_ref[0] % BANDS

    def out_copy(j):
        part = pl.ds(pl.multiple_of(j * (freqs * ROWS), ROWS), freqs * ROWS)
        return pltpu.make_async_copy(moved_ref.at[part, :], stored_ref.at[part, :], sems.at[j])

    def direction(j, sums):
        moment, stress_x, stress_y, drift_x, drift_y, damp_x, damp_y = sums
        cosine, sine = trig_ref[at, j], trig_ref[at, dirs + j]
        start = pl.multiple_of(j * (freqs * ROWS), ROWS)
        second, third, fourth = zero, zero, zero
        for k in range(freqs):
            face = slice(k * ROWS, (k + 1) * ROWS)
            energy = spec_ref[pl.ds(start + k * ROWS, ROWS), :]
            lower = shifted_down(energy) if k == 0 else spec_ref[pl.ds(start + (k * ROWS - 1), ROWS), :]
            u = sx_ref[face, :] * cosine + flow_x
            below = u * jnp.where(u > 0.0, lower, energy)
            flux_ref[k * PITCH : k * PITCH + ROWS, :] = below
            above = flux_ref[k * PITCH + 1 : k * PITCH + ROWS + 1, :]
            v = sy_ref[face, :] * sine + flow_y
            right = v * jnp.where(v > 0.0, energy, next_y(energy))
            w = sw_ref[face, :] * sine + flow_w
            left = w * jnp.where(w > 0.0, pltpu.roll(energy, 1, 1), energy)
            moved = energy - ((above - below) + (right - left))
            moved_ref[pl.ds(start + k * ROWS, ROWS), :] = moved
            second = second * (RATIO_STEP**-2) + moved
            third = third * (RATIO_STEP**-3) + moved
            fourth = fourth * (RATIO_STEP**-4) + moved
        out_copy(j).start()
        second, third, fourth = sea * second, sea * third, sea * fourth
        wind_gain = gain * jnp.maximum(wind_x * cosine + wind_y * sine, 0.0)
        push = wind_gain * second
        drift = third + wind_gain * fourth
        return (
            moment + second,
            stress_x + cosine * push,
            stress_y + sine * push,
            drift_x + cosine * drift,
            drift_y + sine * drift,
            damp_x + cosine * fourth,
            damp_y + sine * fourth,
        )

    moment, stress_x, stress_y, drift_x, drift_y, damp_x, damp_y = lax.fori_loop(0, dirs, direction, (zero,) * 7)
    for c, (main, damped) in enumerate(((stress_x, zero), (stress_y, zero), (drift_x, damp_x), (drift_y, damp_y))):
        parts_ref[c, 0:16, :] = moment
        parts_ref[c, 16:32, :] = main
        parts_ref[c, 32:48, :] = damped
    for j in range(dirs):
        out_copy(j).wait()


def fix_kernel(
    dirs,
    freqs,
    at_ref,
    trig_ref,
    cell_ref,
    from_pair_hbm,
    from_next_hbm,
    to_pair_ref,
    to_next_ref,
    parts_ref,
    out_ref,
    fix_ref,
    behind_ref,
    ahead_ref,
    from_pair_ref,
    from_next_ref,
    sems,
):
    bins = dirs * freqs
    copies = [
        pltpu.make_async_copy(from_pair_hbm, from_pair_ref, sems.at[0]),
        pltpu.make_async_copy(from_next_hbm, from_next_ref, sems.at[1]),
    ]
    for copy in copies:
        copy.start()
    odd, at = at_ref[0] >= BANDS, at_ref[0] % BANDS
    power = lax.broadcasted_iota(jnp.int32, (freqs, LANES), 0).astype(jnp.float32) - (freqs - 1)
    weights = [jnp.exp(power * (p * math.log(RATIO_STEP))) for p in (2, 3, 4)]
    out_ref[...] = parts_ref[...]
    for copy in copies:
        copy.wait()
    faces = (
        (0, 1.0, from_pair_ref, from_next_ref, to_pair_ref, to_next_ref),
        (ROWS - 1, -1.0, to_next_ref, to_pair_ref, from_next_ref, from_pair_ref),
    )
    for side, (row, sign, behind_odd, behind_even, ahead_odd, ahead_even) in enumerate(faces):
        behind_ref[...] = jnp.where(odd, behind_odd[...], behind_even[...])
        ahead_ref[...] = jnp.where(odd, ahead_odd[...], ahead_even[...])
        mask = slice(bins + freqs, bins + freqs + 1)
        opened = (sign * 0.5 * COURANT) * behind_ref[mask, :] * ahead_ref[mask, :]
        flow = opened * cell_ref[48 + side : 49 + side, :]
        speed = opened * (behind_ref[bins : bins + freqs, :] + ahead_ref[bins : bins + freqs, :])
        wind_x, wind_y, gain = (cell_ref[r : r + 1, :] for r in (row, 16 + row, 32 + row))
        moment, stress_x, stress_y, drift_x, drift_y, damp_x, damp_y = (jnp.zeros((1, LANES), jnp.float32),) * 7
        for j in range(dirs):
            cosine, sine = trig_ref[at, j], trig_ref[at, dirs + j]
            u = speed * cosine + flow
            part = slice(j * freqs, (j + 1) * freqs)
            flux = u * jnp.where(sign * u > 0.0, behind_ref[part, :], ahead_ref[part, :])
            fix_ref[side, part, :] = flux
            second, third, fourth = (jnp.sum(w * flux, axis=0, keepdims=True) for w in weights)
            wind_gain = gain * jnp.maximum(wind_x * cosine + wind_y * sine, 0.0)
            push = wind_gain * second
            drift = third + wind_gain * fourth
            moment += second
            stress_x += cosine * push
            stress_y += sine * push
            drift_x += cosine * drift
            drift_y += sine * drift
            damp_x += cosine * fourth
            damp_y += sine * fourth
        for c, (main, damped) in enumerate(((stress_x, None), (stress_y, None), (drift_x, damp_x), (drift_y, damp_y))):
            out_ref[c, row : row + 1, :] += moment
            out_ref[c, 16 + row : 17 + row, :] += main
            if damped is not None:
                out_ref[c, 32 + row : 33 + row, :] += damped


def forcing_kernel(at_ref, parts_ref, damping_ref, out_ref):
    parts = (parts_ref[0] + parts_ref[1]) + (parts_ref[2] + parts_ref[3])
    steepness = STEEP_COEF * parts[0:16]
    damping = DAMP_RATE * steepness / (1.0 + steepness)
    damping_ref[...] = damping
    own = parts[16:32] - damping * parts[32:48]
    own = jnp.where(at_ref[0] % BANDS < 2, 1.0, STOKES_SCALE) * own
    out_ref[...] = jnp.concatenate([own, jnp.zeros((LANES - ROWS, LANES), jnp.float32)], axis=0).T


def update_kernel(dirs, freqs, at_ref, trig_ref, moved_ref, cell_ref, damping_ref, fix_ref, out_ref):
    j, at = pl.program_id(0), at_ref[0] % BANDS
    cosine, sine = trig_ref[at, j], trig_ref[at, dirs + j]
    wind = jnp.maximum(cell_ref[0:16, :] * cosine + cell_ref[16:32, :] * sine, 0.0)
    sea = cell_ref[56:72, :]
    growth = sea * (cell_ref[32:48, :] * wind - damping_ref[...])
    row = lax.broadcasted_iota(jnp.int32, (ROWS, LANES), 0)
    for k in range(freqs):
        ratio = RATIO_STEP ** (k - freqs + 1)
        first, last = (jnp.broadcast_to(fix_ref[side, pl.ds(j * freqs + k, 1), :], (ROWS, LANES)) for side in (0, 1))
        edge = jnp.where(row == 0, first, jnp.where(row == ROWS - 1, last, 0.0))
        moved = moved_ref[k * ROWS : (k + 1) * ROWS, :] + edge
        out_ref[k * ROWS : (k + 1) * ROWS, :] = moved * (sea + ratio * growth)


def row_kernel(got_ref, out_ref):
    lane = lane_of((ROWS, LANES))
    row = got_ref[pl.ds(0, ROWS, stride=8), :]
    for s in range(1, 8):
        row = jnp.where(lane < ROWS * s, row, pltpu.roll(got_ref[pl.ds(s, ROWS, stride=8), :], ROWS * s, 1))
    out_ref[...] = row


def f32(*shape):
    return jax.ShapeDtypeStruct(shape, jnp.float32)


def near(*shape):
    return VMEM(shape, jnp.float32)


def held(value):
    return pltpu.with_memory_space_constraint(value, VMEM)


def one_step(spectrum, group_speed, ocean_current, route_slot, wind_vector, ice_cover):
    dirs, freqs, _, _ = spectrum.shape
    bands, blocks = lax.axis_size(DIR), lax.axis_size(BLK)
    bins = dirs * freqs
    at = (lax.axis_index(DIR) + bands * (lax.axis_index(BLK) & 1)).astype(jnp.int32).reshape(1)
    angles = (2.0 * np.pi * np.arange(bands * dirs, dtype=np.float32) / np.float32(bands * dirs)).astype(np.float32)
    angles = angles.astype(np.float64).reshape(bands, dirs)
    trig = jnp.asarray(np.concatenate([np.cos(angles), np.sin(angles)], axis=1).astype(np.float32))
    smem = pl.BlockSpec(memory_space=SMEM)

    def far(value):
        return pltpu.with_memory_space_constraint(value, pltpu.HBM)

    flat, speed = spectrum.reshape(bins * ROWS, LANES), group_speed.reshape(freqs * ROWS, LANES)
    edge = near(bins + freqs + 8, LANES)
    messages, to_pair, to_next, flat, speed = pl.pallas_call(
        lambda *refs: outgoing_kernel(bins, freqs, *refs),
        out_shape=(
            pltpu.HBM((LANES, LANES), jnp.float32),
            edge,
            edge,
            near(bins * ROWS, LANES),
            near(freqs * ROWS, LANES),
        ),
        in_specs=[smem] + [pl.BlockSpec(memory_space=pltpu.HBM)] * 6,
        out_specs=(pl.BlockSpec(memory_space=pltpu.HBM), *vmem_specs(4)),
        scratch_shapes=[
            VMEM((2, ROWS, LANES), jnp.float32),
            VMEM((2, ROWS * LANES), jnp.float32),
            VMEM((ROWS, LANES), jnp.float32),
            VMEM((ROWS, LANES), jnp.int32),
            VMEM((2, ROWS, LANES), jnp.float32),
            VMEM((LANES, LANES), jnp.float32),
            pltpu.SemaphoreType.DMA((7,)),
        ],
        name="outgoing",
        compiler_params=pltpu.CompilerParams(vmem_limit_bytes=8 * MIB),
    )(
        at,
        far(ocean_current.reshape(2, ROWS, LANES)),
        far(wind_vector.reshape(2, ROWS * LANES)),
        far(ice_cover.reshape(ROWS, LANES)),
        far(flat),
        far(speed),
        far(route_slot),
    )
    pairs = [(i, i + 1) for i in range(0, blocks, 2)]
    nexts = [(i, i + 1) for i in range(1, blocks - 1, 2)]
    got = held(lax.all_to_all(messages, BLK, 0, 0, tiled=True))
    from_next = far(lax.ppermute(to_next, BLK, nexts + [(j, i) for i, j in nexts]))
    from_pair = far(lax.ppermute(to_pair, BLK, pairs + [(j, i) for i, j in pairs]))
    move = pl.pallas_call(
        lambda *refs: move_kernel(dirs, freqs, *refs),
        out_shape=(pltpu.HBM((bins * ROWS, LANES), jnp.float32), near(bands, 48, LANES), near(72, LANES)),
        in_specs=[smem, smem] + vmem_specs(4),
        out_specs=(pl.BlockSpec(memory_space=pltpu.HBM), *vmem_specs(2)),
        scratch_shapes=[
            VMEM((LANES, LANES), jnp.float32),
            VMEM((freqs * ROWS, LANES), jnp.float32),
            VMEM((freqs * ROWS, LANES), jnp.float32),
            VMEM((freqs * ROWS, LANES), jnp.float32),
            VMEM((bins * ROWS, LANES), jnp.float32),
            VMEM((freqs * PITCH, LANES), jnp.float32),
            pltpu.SemaphoreType.DMA((dirs,)),
        ],
        name="move",
        compiler_params=pltpu.CompilerParams(vmem_limit_bytes=8 * MIB),
    )
    moved, parts, cell = move(at, trig, got, flat, speed, route_slot)
    parts, fixes = pl.pallas_call(
        lambda *refs: fix_kernel(dirs, freqs, *refs),
        out_shape=(near(bands, 48, LANES), near(2, bins, LANES)),
        in_specs=[smem, smem] + vmem_specs(1) + [pl.BlockSpec(memory_space=pltpu.HBM)] * 2 + vmem_specs(3),
        out_specs=tuple(vmem_specs(2)),
        scratch_shapes=[VMEM((bins + freqs + 8, LANES), jnp.float32)] * 4 + [pltpu.SemaphoreType.DMA((2,))],
        name="fix",
        compiler_params=pltpu.CompilerParams(vmem_limit_bytes=4 * MIB),
    )(at, trig, cell, from_pair, from_next, to_pair, to_next, parts)

    parts = held(lax.all_to_all(parts, DIR, 0, 0, tiled=True))
    damping, own = pl.pallas_call(
        forcing_kernel,
        out_shape=(near(ROWS, LANES), near(LANES, LANES)),
        in_specs=[smem] + vmem_specs(1),
        out_specs=tuple(vmem_specs(2)),
        name="forcing",
        compiler_params=pltpu.CompilerParams(vmem_limit_bytes=4 * MIB),
    )(at, parts)
    ocean = held(lax.all_to_all(own, BLK, 0, 0, tiled=True))
    result = pl.pallas_call(
        lambda *refs: update_kernel(dirs, freqs, *refs),
        out_shape=f32(bins * ROWS, LANES),
        grid=(dirs,),
        in_specs=[smem, smem, pl.BlockSpec((freqs * ROWS, LANES), lambda j: (j, 0))] + vmem_specs(3),
        out_specs=pl.BlockSpec((freqs * ROWS, LANES), lambda j: (j, 0)),
        name="update",
        compiler_params=pltpu.CompilerParams(vmem_limit_bytes=4 * MIB),
        cost_estimate=pl.CostEstimate(flops=3 * bins * ROWS * LANES, bytes_accessed=8 * bins * ROWS * LANES, transcendentals=0),
    )(at, trig, pltpu.with_memory_space_constraint(moved, pltpu.HBM), cell, damping, fixes)
    ocean = pl.pallas_call(
        row_kernel,
        out_shape=f32(ROWS, LANES),
        in_specs=vmem_specs(1),
        out_specs=vmem_specs(1)[0],
        name="rows",
        compiler_params=pltpu.CompilerParams(vmem_limit_bytes=4 * MIB),
    )(ocean)
    return (result.reshape(spectrum.shape), ocean.reshape(1, 1, ROWS * LANES))


def solution(mesh):
    return jax.shard_map(
        one_step,
        mesh=mesh,
        in_specs=(
            P(DIR, None, BLK, None),
            P(None, BLK, None),
            P(None, BLK, None),
            P(BLK, None),
            P(BLK, None, None),
            P(BLK, None),
        ),
        out_specs=(P(DIR, None, BLK, None), P(DIR, BLK, None)),
        check_vma=False,
    )
```

```python
import math

import jax
import jax.numpy as jnp
import numpy as np
from jax import lax
from jax.experimental import pallas as pl
from jax.experimental.pallas import tpu as pltpu
from jax.sharding import PartitionSpec as P


BLK = "blk"
DIR = "dir"
VMEM = pltpu.VMEM
SMEM = pltpu.SMEM

COURANT = 0.15
WIND_GROWTH = 0.15
DAMP_RATE = 0.5
STEEP_COEF = 0.01
STOKES_SCALE = 0.15
RATIO_STEP = 1.1

LANES = 128
BANDS = 4
MIB = 1 << 20
FACES = 36
PITCH = 24
ROWS = 16
CUR_X, CUR_Y, WIND_X, WIND_Y, ICE = 0, 24, 48, 64, 80


def vmem_specs(count):
    return [pl.BlockSpec(memory_space=VMEM)] * count


def lane_of(shape):
    return lax.broadcasted_iota(jnp.int32, shape, len(shape) - 1)


def outgoing_kernel(
    bins,
    freqs,
    at_ref,
    cur_hbm,
    wind_hbm,
    ice_hbm,
    spec_hbm,
    speed_hbm,
    slot_hbm,
    sent_hbm,
    pair_ref,
    next_ref,
    spec_ref,
    speed_ref,
    cur_ref,
    wind_ref,
    ice_ref,
    slot_ref,
    x_ref,
    out_ref,
    sems,
):
    cut = bins // 24 * 8
    starts = (0, cut, 2 * cut, bins)
    parts = [pl.ds(a * ROWS, (b - a) * ROWS) for a, b in zip(starts, starts[1:])]
    sources = (cur_hbm, wind_hbm, ice_hbm, slot_hbm, speed_hbm, *(spec_hbm.at[p, :] for p in parts))
    targets = (cur_ref, wind_ref, ice_ref, slot_ref, speed_ref, *(spec_ref.at[p, :] for p in parts))
    copies = [pltpu.make_async_copy(a, b, sems.at[i]) for i, (a, b) in enumerate(zip(sources, targets))]
    for copy in copies:
        copy.start()
    for copy in copies[:3]:
        copy.wait()
    for c in range(2):
        for r in range(ROWS):
            x_ref[c, r : r + 1, :] = wind_ref[c : c + 1, LANES * r : LANES * (r + 1)]
    lane = lane_of((ROWS, LANES))

    def put(s, values, start):
        return pltpu.roll(values, (start - ROWS * s) % LANES, 1)

    for s in range(8):
        row = jnp.where(lane < CUR_Y, put(s, cur_ref[0], CUR_X + 1), put(s, cur_ref[1], CUR_Y))
        row = jnp.where(lane < WIND_X, row, put(s, x_ref[0], WIND_X))
        row = jnp.where(lane < WIND_Y, row, put(s, x_ref[1], WIND_Y))
        row = jnp.where(lane < ICE, row, put(s, ice_ref[...], ICE))
        out_ref[pl.ds(s, ROWS, stride=8), :] = row
    whole = out_ref[...]
    wide = lane_of((LANES, LANES))
    before = pltpu.roll(pltpu.roll(whole, 1, 0), LANES - ROWS, 1)
    after = pltpu.roll(pltpu.roll(whole, LANES - 1, 0), ROWS, 1)
    whole = jnp.where(wide == CUR_X, before, whole)
    out_ref[...] = jnp.where(wide == CUR_X + ROWS + 1, after, whole)
    sending = pltpu.make_async_copy(out_ref, sent_hbm, sems.at[len(sources)])
    sending.start()
    odd = at_ref[0] >= BANDS

    def trade(start, stop, first, last):
        pair_ref[start:stop, :] = jnp.where(odd, first, last)
        next_ref[start:stop, :] = jnp.where(odd, last, first)

    def rows_of(source, start, count, row):
        return source[pl.ds(start * ROWS + row, count, stride=ROWS), :]

    copies[3].wait()
    sea = jnp.where(slot_ref[...] >= 0, 1.0, 0.0)
    sea = [jnp.broadcast_to(sea[r : r + 1, :], (8, LANES)) for r in (0, ROWS - 1)]
    trade(bins + freqs, bins + freqs + 8, *sea)
    copies[4].wait()
    trade(bins, bins + freqs, *(rows_of(speed_ref, 0, freqs, r) for r in (0, ROWS - 1)))
    for copy, start, stop in zip(copies[5:], starts, starts[1:]):
        copy.wait()
        trade(start, stop, *(rows_of(spec_ref, start, stop - start, r) for r in (0, ROWS - 1)))
    sending.wait()


def move_kernel(
    dirs,
    freqs,
    at_ref,
    trig_ref,
    got_ref,
    spec_ref,
    speed_ref,
    slot_ref,
    stored_ref,
    parts_ref,
    cell_ref,
    turned_ref,
    sx_ref,
    sy_ref,
    sw_ref,
    moved_ref,
    flux_ref,
    sems,
):
    shape = (ROWS, LANES)
    row, lane = lax.broadcasted_iota(jnp.int32, shape, 0), lane_of(shape)
    turned_ref[...] = got_ref[...].T

    def shifted_down(values):
        return pltpu.roll(values, 1, 0)

    def next_y(values):
        return pltpu.roll(values, LANES - 1, 1)

    slots = slot_ref[...]
    sea = jnp.where(slots >= 0, 1.0, 0.0)
    half = 0.5 * COURANT
    open_x = jnp.where(row > 0, half * sea * shifted_down(sea), 0.0)
    open_y = jnp.where(lane < LANES - 1, half * sea * next_y(sea), 0.0)
    flow_x = open_x * (turned_ref[CUR_X : CUR_X + ROWS, :] + turned_ref[CUR_X + 1 : CUR_X + ROWS + 1, :])
    cur_y = turned_ref[CUR_Y : CUR_Y + ROWS, :]
    flow_y = open_y * (cur_y + next_y(cur_y))
    flow_w = pltpu.roll(flow_y, 1, 1)
    open_w = pltpu.roll(open_y, 1, 1)

    owner, place = jnp.maximum(slots, 0) // 16, jnp.where(slots >= 0, slots % 16, -1)
    wind_x, wind_y, ice = (jnp.zeros(shape, jnp.float32) for _ in range(3))
    for s in range(16):
        here = place == s

        def picked(start, old):
            table = jnp.broadcast_to(turned_ref[start + s : start + s + 1, :], shape)
            return jnp.where(here, jnp.take_along_axis(table, owner, axis=1), old)

        wind_x, wind_y, ice = picked(WIND_X, wind_x), picked(WIND_Y, wind_y), picked(ICE, ice)
    gain = WIND_GROWTH * (1.0 - ice)
    cell_ref[0:16, :] = wind_x
    cell_ref[16:32, :] = wind_y
    cell_ref[32:48, :] = gain
    cell_ref[56:72, :] = sea
    for side, x in enumerate((CUR_X, CUR_X + ROWS)):
        cell_ref[48 + side : 49 + side, :] = turned_ref[x : x + 1, :] + turned_ref[x + 1 : x + 2, :]

    def faces(k, _):
        base = pl.multiple_of(k * ROWS, ROWS)
        speed = speed_ref[pl.ds(base, ROWS), :]
        sx_ref[pl.ds(base, ROWS), :] = open_x * (speed + shifted_down(speed))
        sy_ref[pl.ds(base, ROWS), :] = open_y * (speed + next_y(speed))
        sw_ref[pl.ds(base, ROWS), :] = open_w * (speed + pltpu.roll(speed, 1, 1))
        return 0

    lax.fori_loop(0, freqs, faces, 0, unroll=FACES)

    zero = jnp.zeros(shape, jnp.float32)
    for k in range(freqs):
        flux_ref[k * PITCH + ROWS : (k + 1) * PITCH, :] = jnp.zeros((PITCH - ROWS, LANES), jnp.float32)
    at = at_ref[0] % BANDS

    def out_copy(j):
        part = pl.ds(pl.multiple_of(j * (freqs * ROWS), ROWS), freqs * ROWS)
        return pltpu.make_async_copy(moved_ref.at[part, :], stored_ref.at[part, :], sems.at[j])

    def direction(j, sums):
        moment, stress_x, stress_y, drift_x, drift_y, damp_x, damp_y = sums
        cosine, sine = trig_ref[at, j], trig_ref[at, dirs + j]
        start = pl.multiple_of(j * (freqs * ROWS), ROWS)
        second, third, fourth = zero, zero, zero
        for k in range(freqs):
            face = slice(k * ROWS, (k + 1) * ROWS)
            energy = spec_ref[pl.ds(start + k * ROWS, ROWS), :]
            lower = shifted_down(energy) if k == 0 else spec_ref[pl.ds(start + (k * ROWS - 1), ROWS), :]
            u = sx_ref[face, :] * cosine + flow_x
            below = u * jnp.where(u > 0.0, lower, energy)
            flux_ref[k * PITCH : k * PITCH + ROWS, :] = below
            above = flux_ref[k * PITCH + 1 : k * PITCH + ROWS + 1, :]
            v = sy_ref[face, :] * sine + flow_y
            right = v * jnp.where(v > 0.0, energy, next_y(energy))
            w = sw_ref[face, :] * sine + flow_w
            left = w * jnp.where(w > 0.0, pltpu.roll(energy, 1, 1), energy)
            moved = energy - ((above - below) + (right - left))
            moved_ref[pl.ds(start + k * ROWS, ROWS), :] = moved
            second = second * (RATIO_STEP**-2) + moved
            third = third * (RATIO_STEP**-3) + moved
            fourth = fourth * (RATIO_STEP**-4) + moved
        out_copy(j).start()
        second, third, fourth = sea * second, sea * third, sea * fourth
        wind_gain = gain * jnp.maximum(wind_x * cosine + wind_y * sine, 0.0)
        push = wind_gain * second
        drift = third + wind_gain * fourth
        return (
            moment + second,
            stress_x + cosine * push,
            stress_y + sine * push,
            drift_x + cosine * drift,
            drift_y + sine * drift,
            damp_x + cosine * fourth,
            damp_y + sine * fourth,
        )

    moment, stress_x, stress_y, drift_x, drift_y, damp_x, damp_y = lax.fori_loop(0, dirs, direction, (zero,) * 7)
    for c, (main, damped) in enumerate(((stress_x, zero), (stress_y, zero), (drift_x, damp_x), (drift_y, damp_y))):
        parts_ref[c, 0:16, :] = moment
        parts_ref[c, 16:32, :] = main
        parts_ref[c, 32:48, :] = damped
    for j in range(dirs):
        out_copy(j).wait()


def fix_kernel(
    dirs,
    freqs,
    at_ref,
    trig_ref,
    cell_ref,
    from_pair_ref,
    from_next_ref,
    to_pair_ref,
    to_next_ref,
    parts_ref,
    out_ref,
    fix_ref,
    behind_ref,
    ahead_ref,
):
    bins = dirs * freqs
    odd, at = at_ref[0] >= BANDS, at_ref[0] % BANDS
    power = lax.broadcasted_iota(jnp.int32, (freqs, LANES), 0).astype(jnp.float32) - (freqs - 1)
    weights = [jnp.exp(power * (p * math.log(RATIO_STEP))) for p in (2, 3, 4)]
    out_ref[...] = parts_ref[...]
    faces = (
        (0, 1.0, from_pair_ref, from_next_ref, to_pair_ref, to_next_ref),
        (ROWS - 1, -1.0, to_next_ref, to_pair_ref, from_next_ref, from_pair_ref),
    )
    for side, (row, sign, behind_odd, behind_even, ahead_odd, ahead_even) in enumerate(faces):
        behind_ref[...] = jnp.where(odd, behind_odd[...], behind_even[...])
        ahead_ref[...] = jnp.where(odd, ahead_odd[...], ahead_even[...])
        mask = slice(bins + freqs, bins + freqs + 1)
        opened = (sign * 0.5 * COURANT) * behind_ref[mask, :] * ahead_ref[mask, :]
        flow = opened * cell_ref[48 + side : 49 + side, :]
        speed = opened * (behind_ref[bins : bins + freqs, :] + ahead_ref[bins : bins + freqs, :])
        wind_x, wind_y, gain = (cell_ref[r : r + 1, :] for r in (row, 16 + row, 32 + row))
        moment, stress_x, stress_y, drift_x, drift_y, damp_x, damp_y = (jnp.zeros((1, LANES), jnp.float32),) * 7
        for j in range(dirs):
            cosine, sine = trig_ref[at, j], trig_ref[at, dirs + j]
            u = speed * cosine + flow
            part = slice(j * freqs, (j + 1) * freqs)
            flux = u * jnp.where(sign * u > 0.0, behind_ref[part, :], ahead_ref[part, :])
            fix_ref[side, part, :] = flux
            second, third, fourth = (jnp.sum(w * flux, axis=0, keepdims=True) for w in weights)
            wind_gain = gain * jnp.maximum(wind_x * cosine + wind_y * sine, 0.0)
            push = wind_gain * second
            drift = third + wind_gain * fourth
            moment += second
            stress_x += cosine * push
            stress_y += sine * push
            drift_x += cosine * drift
            drift_y += sine * drift
            damp_x += cosine * fourth
            damp_y += sine * fourth
        for c, (main, damped) in enumerate(((stress_x, None), (stress_y, None), (drift_x, damp_x), (drift_y, damp_y))):
            out_ref[c, row : row + 1, :] += moment
            out_ref[c, 16 + row : 17 + row, :] += main
            if damped is not None:
                out_ref[c, 32 + row : 33 + row, :] += damped


def forcing_kernel(at_ref, parts_ref, damping_ref, out_ref):
    parts = (parts_ref[0] + parts_ref[1]) + (parts_ref[2] + parts_ref[3])
    steepness = STEEP_COEF * parts[0:16]
    damping = DAMP_RATE * steepness / (1.0 + steepness)
    damping_ref[...] = damping
    own = parts[16:32] - damping * parts[32:48]
    own = jnp.where(at_ref[0] % BANDS < 2, 1.0, STOKES_SCALE) * own
    out_ref[...] = jnp.concatenate([own, jnp.zeros((LANES - ROWS, LANES), jnp.float32)], axis=0).T


def update_kernel(dirs, freqs, at_ref, trig_ref, moved_ref, cell_ref, damping_ref, fix_ref, out_ref):
    j, at = pl.program_id(0), at_ref[0] % BANDS
    cosine, sine = trig_ref[at, j], trig_ref[at, dirs + j]
    wind = jnp.maximum(cell_ref[0:16, :] * cosine + cell_ref[16:32, :] * sine, 0.0)
    sea = cell_ref[56:72, :]
    growth = sea * (cell_ref[32:48, :] * wind - damping_ref[...])
    row = lax.broadcasted_iota(jnp.int32, (ROWS, LANES), 0)
    for k in range(freqs):
        ratio = RATIO_STEP ** (k - freqs + 1)
        first, last = (jnp.broadcast_to(fix_ref[side, pl.ds(j * freqs + k, 1), :], (ROWS, LANES)) for side in (0, 1))
        edge = jnp.where(row == 0, first, jnp.where(row == ROWS - 1, last, 0.0))
        moved = moved_ref[k * ROWS : (k + 1) * ROWS, :] + edge
        out_ref[k * ROWS : (k + 1) * ROWS, :] = moved * (sea + ratio * growth)


def row_kernel(got_ref, out_ref):
    lane = lane_of((ROWS, LANES))
    row = got_ref[pl.ds(0, ROWS, stride=8), :]
    for s in range(1, 8):
        row = jnp.where(lane < ROWS * s, row, pltpu.roll(got_ref[pl.ds(s, ROWS, stride=8), :], ROWS * s, 1))
    out_ref[...] = row


def f32(*shape):
    return jax.ShapeDtypeStruct(shape, jnp.float32)


def near(*shape):
    return VMEM(shape, jnp.float32)


def held(value):
    return pltpu.with_memory_space_constraint(value, VMEM)


def one_step(spectrum, group_speed, ocean_current, route_slot, wind_vector, ice_cover):
    dirs, freqs, _, _ = spectrum.shape
    bands, blocks = lax.axis_size(DIR), lax.axis_size(BLK)
    bins = dirs * freqs
    at = (lax.axis_index(DIR) + bands * (lax.axis_index(BLK) & 1)).astype(jnp.int32).reshape(1)
    angles = (2.0 * np.pi * np.arange(bands * dirs, dtype=np.float32) / np.float32(bands * dirs)).astype(np.float32)
    angles = angles.astype(np.float64).reshape(bands, dirs)
    trig = jnp.asarray(np.concatenate([np.cos(angles), np.sin(angles)], axis=1).astype(np.float32))
    smem = pl.BlockSpec(memory_space=SMEM)

    def far(value):
        return pltpu.with_memory_space_constraint(value, pltpu.HBM)

    flat, speed = spectrum.reshape(bins * ROWS, LANES), group_speed.reshape(freqs * ROWS, LANES)
    edge = near(bins + freqs + 8, LANES)
    messages, to_pair, to_next, flat, speed = pl.pallas_call(
        lambda *refs: outgoing_kernel(bins, freqs, *refs),
        out_shape=(
            pltpu.HBM((LANES, LANES), jnp.float32),
            edge,
            edge,
            near(bins * ROWS, LANES),
            near(freqs * ROWS, LANES),
        ),
        in_specs=[smem] + [pl.BlockSpec(memory_space=pltpu.HBM)] * 6,
        out_specs=(pl.BlockSpec(memory_space=pltpu.HBM), *vmem_specs(4)),
        scratch_shapes=[
            VMEM((2, ROWS, LANES), jnp.float32),
            VMEM((2, ROWS * LANES), jnp.float32),
            VMEM((ROWS, LANES), jnp.float32),
            VMEM((ROWS, LANES), jnp.int32),
            VMEM((2, ROWS, LANES), jnp.float32),
            VMEM((LANES, LANES), jnp.float32),
            pltpu.SemaphoreType.DMA((9,)),
        ],
        name="outgoing",
        compiler_params=pltpu.CompilerParams(vmem_limit_bytes=8 * MIB),
    )(
        at,
        far(ocean_current.reshape(2, ROWS, LANES)),
        far(wind_vector.reshape(2, ROWS * LANES)),
        far(ice_cover.reshape(ROWS, LANES)),
        far(flat),
        far(speed),
        far(route_slot),
    )
    pairs = [(i, i + 1) for i in range(0, blocks, 2)]
    nexts = [(i, i + 1) for i in range(1, blocks - 1, 2)]
    got = held(lax.all_to_all(messages, BLK, 0, 0, tiled=True))
    from_next = held(lax.ppermute(to_next, BLK, nexts + [(j, i) for i, j in nexts]))
    from_pair = held(lax.ppermute(to_pair, BLK, pairs + [(j, i) for i, j in pairs]))
    move = pl.pallas_call(
        lambda *refs: move_kernel(dirs, freqs, *refs),
        out_shape=(pltpu.HBM((bins * ROWS, LANES), jnp.float32), near(bands, 48, LANES), near(72, LANES)),
        in_specs=[smem, smem] + vmem_specs(4),
        out_specs=(pl.BlockSpec(memory_space=pltpu.HBM), *vmem_specs(2)),
        scratch_shapes=[
            VMEM((LANES, LANES), jnp.float32),
            VMEM((freqs * ROWS, LANES), jnp.float32),
            VMEM((freqs * ROWS, LANES), jnp.float32),
            VMEM((freqs * ROWS, LANES), jnp.float32),
            VMEM((bins * ROWS, LANES), jnp.float32),
            VMEM((freqs * PITCH, LANES), jnp.float32),
            pltpu.SemaphoreType.DMA((dirs,)),
        ],
        name="move",
        compiler_params=pltpu.CompilerParams(vmem_limit_bytes=8 * MIB),
    )
    moved, parts, cell = move(at, trig, got, flat, speed, route_slot)
    parts, fixes = pl.pallas_call(
        lambda *refs: fix_kernel(dirs, freqs, *refs),
        out_shape=(near(bands, 48, LANES), near(2, bins, LANES)),
        in_specs=[smem, smem] + vmem_specs(6),
        out_specs=tuple(vmem_specs(2)),
        scratch_shapes=[VMEM((bins + freqs + 8, LANES), jnp.float32), VMEM((bins + freqs + 8, LANES), jnp.float32)],
        name="fix",
        compiler_params=pltpu.CompilerParams(vmem_limit_bytes=4 * MIB),
    )(at, trig, cell, from_pair, from_next, to_pair, to_next, parts)

    parts = held(lax.all_to_all(parts, DIR, 0, 0, tiled=True))
    damping, own = pl.pallas_call(
        forcing_kernel,
        out_shape=(near(ROWS, LANES), near(LANES, LANES)),
        in_specs=[smem] + vmem_specs(1),
        out_specs=tuple(vmem_specs(2)),
        name="forcing",
        compiler_params=pltpu.CompilerParams(vmem_limit_bytes=4 * MIB),
    )(at, parts)
    ocean = held(lax.all_to_all(own, BLK, 0, 0, tiled=True))
    result = pl.pallas_call(
        lambda *refs: update_kernel(dirs, freqs, *refs),
        out_shape=f32(bins * ROWS, LANES),
        grid=(dirs,),
        in_specs=[smem, smem, pl.BlockSpec((freqs * ROWS, LANES), lambda j: (j, 0))] + vmem_specs(3),
        out_specs=pl.BlockSpec((freqs * ROWS, LANES), lambda j: (j, 0)),
        name="update",
        compiler_params=pltpu.CompilerParams(vmem_limit_bytes=4 * MIB),
        cost_estimate=pl.CostEstimate(flops=3 * bins * ROWS * LANES, bytes_accessed=8 * bins * ROWS * LANES, transcendentals=0),
    )(at, trig, pltpu.with_memory_space_constraint(moved, pltpu.HBM), cell, damping, fixes)
    ocean = pl.pallas_call(
        row_kernel,
        out_shape=f32(ROWS, LANES),
        in_specs=vmem_specs(1),
        out_specs=vmem_specs(1)[0],
        name="rows",
        compiler_params=pltpu.CompilerParams(vmem_limit_bytes=4 * MIB),
    )(ocean)
    return (result.reshape(spectrum.shape), ocean.reshape(1, 1, ROWS * LANES))


def solution(mesh):
    return jax.shard_map(
        one_step,
        mesh=mesh,
        in_specs=(
            P(DIR, None, BLK, None),
            P(None, BLK, None),
            P(None, BLK, None),
            P(BLK, None),
            P(BLK, None, None),
            P(BLK, None),
        ),
        out_specs=(P(DIR, None, BLK, None), P(DIR, BLK, None)),
        check_vma=False,
    )
```
